256 devices in a mesh: cfg: 2 (over core), seq: 32 (over y, z), blk: 4 (over x).
Axes of the slice: x: 4, y: 4, z: 8, core: 2. Of those that a mesh axis runs over, the one named last changes fastest.
Arguments:
- queries: bfloat16 [2, 12288, 1536], P('cfg', 'seq', 'blk'), may hold values from -20 to 20
- keys: bfloat16 [2, 12288, 1536], P('cfg', 'seq', 'blk'), may hold values from -20 to 20
- values: bfloat16 [2, 12288, 1536], P('cfg', 'seq', 'blk'), may hold values from -6 to 6
- residual: bfloat16 [2, 12288, 1536], P('cfg', 'seq'), may hold values from -6 to 6
- w_out: bfloat16 [1536, 1536], P('blk'), may hold values from -0.15625 to 0.15625
- w_up: bfloat16 [1536, 6144], P(None, 'blk'), may hold values from -0.15625 to 0.15625
- w_down: bfloat16 [6144, 1536], P('blk'), may hold values from -0.078125 to 0.078125
- modulation: float32 [3, 4, 1536], replicated, may hold values from -3 to 3
- guide_scale: float32 [3], replicated, may hold values from 1.5 to 4
- slot_clip: int32 [12288], P('seq'), may hold values from 0 to 3, as said below
- owner: int32 [12288, 1], P('seq'), may hold values from 0 to 31; in each aligned block of 192 rows (0 to 191, 192 to 383, ...) at most 12 rows name the same one
Outputs:
- returned: bfloat16 [2, 12288, 1536], P('cfg', 'seq', 'blk')
The draws below stay inside these ranges and needn't reach their ends.
Inputs may be any that keep to these rules, and one draw needn't show every extreme that they name: `slot_clip`: each device's block of 384 slots holds its live slots first and its padding slots, marked 3, last; live slots, counted block after block, are dealt to the clips in turn (the t-th live slot belongs to clip t mod 3), so each clip has 3584 live slots. In each aligned half-block of 192 slots no owner is named more than 12 times.
All inputs are finite; a program needn't handle non-finite values.
Results may differ from the reference program's by a relative error of at most 0.017.
Values may be sent and summed in bfloat16 or wider, within the bound.
A program may use at most 128 MiB of HBM per device.

```python
import math
import jax
import jax.numpy as jnp
import numpy as np
from jax import lax

D = 1536
HEADS = 12
HEAD_DIM = 128
FFW = 6144
CLIPS = 3
SLOTS = 384
PAD_DEV = 48
HALF = 192
ROWS = 12288
CAP = 12
OUT_ROWS = 12288
N_SEQ = 32


def draw_queries(key, part):
    result = jnp.clip(1.6 * jax.random.normal(jax.random.fold_in(key, 21), (2, ROWS, D), jnp.float32), -9.6, 9.6)
    return result.astype(jnp.bfloat16)


def draw_keys(key, part):
    result = jnp.clip(1.6 * jax.random.normal(jax.random.fold_in(key, 22), (2, ROWS, D), jnp.float32), -9.6, 9.6)
    return result.astype(jnp.bfloat16)


def draw_slot_clip(key, part):
    blocks = ROWS // SLOTS
    swing = jax.random.randint(jax.random.fold_in(key, 1), (blocks // 2,), -PAD_DEV, PAD_DEV + 1)
    order = jax.random.permutation(jax.random.fold_in(key, 2), blocks)
    padding = PAD_DEV + jnp.concatenate([swing, -swing])[order]
    filled = SLOTS - padding
    starts = jnp.cumsum(filled) - filled
    position = jnp.arange(SLOTS)
    token = starts[:, None] + position[None, :]
    clip_id = jnp.where(position[None, :] < filled[:, None], token % CLIPS, CLIPS)
    return clip_id.reshape(ROWS).astype(jnp.int32)


def level_of(key, extent, cuts, least, top_value):
    factor_of = 1.0
    for dim, blocks in cuts:
        draws = jax.random.uniform(jax.random.fold_in(jax.random.fold_in(key, 6), dim), (blocks,), jnp.float32, least / len(cuts), top_value / len(cuts))
        factor_of = factor_of * jnp.repeat(jnp.exp(draws), extent[dim] // blocks).reshape((-1,) + (1,) * (len(extent) - 1 - dim))
    return factor_of


def deal_out(stream_key, own, number, rows, amount, top, bound, slope):
    order = jax.random.permutation(stream_key, amount)
    packed, usual = portions_of(amount, rows * top, bound, slope, True), portions_of(amount, rows * top, bound, slope, False)
    places = jnp.arange(amount)

    def named(lengths, offset_by):
        used = int((lengths > 0).sum())
        fixed = max(1, used // 4)
        shifted = fixed + (places - fixed + offset_by * (used - fixed)) % max(1, amount - fixed)
        return jnp.zeros((amount,), jnp.int32).at[order[jnp.where(places < fixed, places, shifted)]].set(jnp.asarray(lengths, jnp.int32))

    lengths = jnp.where(number % 4 == 0, named(packed, number // 4), named(usual, number - number // 4 - 1))
    mixed = jax.random.permutation(jax.random.fold_in(own, 3), amount)
    donor, receiver = mixed[0:amount // 2 * 2:2], mixed[1:amount // 2 * 2:2]
    margin = jnp.minimum(lengths[donor] - 1, bound - lengths[receiver]) // 2
    margin = jnp.where((donor == order[0]) | (receiver == order[0]) | (lengths[receiver] == 0), 0, jnp.maximum(margin, 0))
    shifted = jax.random.randint(jax.random.fold_in(own, 4), (amount // 2,), 0, 1 << 20) % (margin + 1)
    lengths = lengths.at[donor].add(-shifted).at[receiver].add(shifted)
    labels = jnp.searchsorted(jnp.cumsum(lengths), jnp.arange(rows * top), side="right").astype(jnp.int32)
    table = labels.reshape(top, rows).T
    table = table[jax.random.permutation(jax.random.fold_in(own, 1), rows)]
    offset_by = jax.random.randint(jax.random.fold_in(own, 2), (rows, 1), 0, top)
    return jnp.take_along_axis(table, (jnp.arange(top)[None, :] + offset_by) % top, axis=1)


def portions_of(count, total, reach, lean, full):
    portions = [(1 << 20) // math.isqrt(grade ** lean) + 1 for grade in range(1, count + 1)]
    largest = reach if full else min(reach, max(-(-total // count), total * portions[0] // sum(portions)))
    least = 1 if total - largest >= count - 1 else 0
    counts, surplus = [largest] + [least] * (count - 1), total - largest - least * (count - 1)
    while surplus > 0:
        candidates = [i for i in range(1, count) if counts[i] < largest] or [i for i in range(1, count) if counts[i] < reach]
        pool, left = sum([portions[i] for i in candidates]), surplus
        for i in candidates:
            extra = min(reach - counts[i], max(1, left * portions[i] // pool), surplus)
            counts[i] = counts[i] + extra
            surplus = surplus - extra
    return np.array(counts)


def noise(stream_key, extent, scale, reach, shards=(), held_as=jnp.bfloat16):
    values = scale * jax.random.normal(stream_key, extent, jnp.float32)
    if shards:
        values = values * level_of(stream_key, extent, shards, -0.22, 0.18)
    return jnp.clip(values, -reach, reach).astype(held_as)


def setup_inputs(seed: int = 0) -> dict:
    key_list = jax.random.split(jax.random.key(seed), 12)
    queries = draw_queries(jax.random.fold_in(key_list[11], 71), 0)
    keys = draw_keys(jax.random.fold_in(key_list[11], 71), 0)
    values = noise(key_list[2], (2, ROWS, D), 1.0, 6.0, ((0, 2), (1, 32), (2, 4)))
    residual = noise(key_list[3], (2, ROWS, D), 1.0, 6.0, ((0, 2), (1, 32)))
    w_out = noise(key_list[4], (D, D), D ** -0.5, 0.15625, ((0, 4),))
    w_up = noise(key_list[5], (D, FFW), D ** -0.5, 0.15625, ((1, 4),))
    w_down = noise(key_list[6], (FFW, D), FFW ** -0.5, 0.078125, ((0, 4),))
    modulation = noise(key_list[7], (CLIPS, 4, D), 0.5, 3.0, (), jnp.float32)
    guide_scale = jnp.clip(jax.random.uniform(key_list[8], (CLIPS,), jnp.float32, 1.5, 4.0), 1.5, 4.0)
    slot_clip = draw_slot_clip(jax.random.fold_in(key_list[11], 71), 0)
    owner_keys = jax.random.split(jax.random.fold_in(key_list[10], 1), ROWS // HALF)
    owner_turns = jax.random.permutation(jax.random.fold_in(key_list[10], 3), ROWS // HALF)
    owner = jax.vmap(lambda own, number: deal_out(jax.random.fold_in(key_list[10], 2), own, number, HALF, N_SEQ, 1, CAP, 1))(owner_keys, owner_turns).reshape((ROWS, 1))
    return {"queries": queries, "keys": keys, "values": values, "residual": residual, "w_out": w_out, "w_up": w_up, "w_down": w_down, "modulation": modulation, "guide_scale": guide_scale, "slot_clip": slot_clip, "owner": owner}


NEG_FILL = -1e+30

def reference(queries, keys, values, residual, w_out, w_up, w_down, modulation, guide_scale, slot_clip, owner):
    live = slot_clip < CLIPS
    factor = 1.0 / math.sqrt(HEAD_DIM)

    def split_heads(tensor):
        return tensor.reshape(2, ROWS, HEADS, HEAD_DIM).transpose(0, 2, 1, 3).reshape(2 * HEADS, ROWS, HEAD_DIM)

    def attend_group(group):
        query_rows, key_rows, value_rows = group

        def one_block(block):
            start = (block * SLOTS).astype(jnp.int32)
            query_block = lax.dynamic_slice_in_dim(query_rows, start, SLOTS, 0)
            clip_block = lax.dynamic_slice_in_dim(slot_clip, start, SLOTS, 0)
            scores = jnp.dot(query_block, key_rows.T, preferred_element_type=jnp.float32) * factor
            kept = (slot_clip[None, :] == clip_block[:, None]) & (clip_block[:, None] < CLIPS)
            scores = jnp.where(kept, scores, NEG_FILL)
            peak = lax.optimization_barrier(jnp.max(scores, axis=1, keepdims=True))
            weights = jnp.exp(scores - peak)
            totals = lax.optimization_barrier(jnp.sum(weights, axis=1, keepdims=True))
            summed = jnp.dot(weights.astype(jnp.bfloat16), value_rows, preferred_element_type=jnp.float32)
            return summed / totals
        blocks = lax.map(one_block, jnp.arange(ROWS // SLOTS, dtype=jnp.int32))
        return blocks.reshape(ROWS, HEAD_DIM)
    attended = lax.map(attend_group, (split_heads(queries), split_heads(keys), split_heads(values)))
    attended = attended.reshape(2, HEADS, ROWS, HEAD_DIM).transpose(0, 2, 1, 3).reshape(2, ROWS, D)
    attended = jnp.where(live[None, :, None], attended, 0.0).astype(jnp.bfloat16)
    projected = jnp.dot(attended.reshape(2 * ROWS, D), w_out, preferred_element_type=jnp.float32).reshape(2, ROWS, D)
    table = jnp.concatenate([modulation, jnp.zeros((1, 4, D), jnp.float32)], axis=0)
    row_mod = table[slot_clip]
    gate_attn = row_mod[None, :, 0]
    shift = row_mod[None, :, 1]
    stretch = row_mod[None, :, 2]
    gate_mlp = row_mod[None, :, 3]
    mixed = residual.astype(jnp.float32) + gate_attn * projected
    centre = mixed - lax.optimization_barrier(jnp.mean(mixed, axis=-1, keepdims=True))
    spread = lax.optimization_barrier(jnp.mean(centre * centre, axis=-1, keepdims=True))
    normed = (centre * lax.rsqrt(spread + 1e-06) * (1.0 + stretch) + shift).astype(jnp.bfloat16)
    hidden = jax.nn.gelu(jnp.dot(normed.reshape(2 * ROWS, D), w_up, preferred_element_type=jnp.float32), approximate=True).astype(jnp.bfloat16)
    feed = jnp.dot(hidden, w_down, preferred_element_type=jnp.float32).reshape(2, ROWS, D)
    block_out = (mixed + gate_mlp * feed).astype(jnp.bfloat16)
    cond = block_out[0].astype(jnp.float32)
    uncond = block_out[1].astype(jnp.float32)
    strength = jnp.concatenate([guide_scale, jnp.zeros((1,), jnp.float32)])[slot_clip]
    guided = jnp.where(live[:, None], uncond + strength[:, None] * (cond - uncond), 0.0).astype(jnp.bfloat16)
    owned = owner[:, 0].reshape(N_SEQ, 2, HALF)
    onehot = (owned[..., None] == jnp.arange(N_SEQ, dtype=jnp.int32)).astype(jnp.int32)
    rank = lax.optimization_barrier(jnp.sum((jnp.cumsum(onehot, axis=2) - onehot) * onehot, axis=-1))
    source = jnp.arange(N_SEQ, dtype=jnp.int32)[:, None, None]
    halfid = jnp.arange(2, dtype=jnp.int32)[None, :, None]
    target = (((halfid * N_SEQ + owned) * N_SEQ + source) * CAP + rank).astype(jnp.int32)
    returned = jnp.zeros((2 * OUT_ROWS, D), jnp.bfloat16).at[target.reshape(-1)].set(guided.reshape(ROWS, D))
    return returned.reshape(2, OUT_ROWS, D)
```

```python
import functools
import math

import jax
import jax.numpy as jnp
from jax import lax
from jax.experimental import pallas as pl
from jax.experimental.pallas import tpu as pltpu
from jax.sharding import PartitionSpec as P

D = 1536
HEAD_DIM = 128
CLIPS = 3
HEADS_HERE = 3
GROUP = 128
Y, Z = 4, 8
MSG = 400
KV = pl.ds(128, 272)
NEG_FILL = -1e30
EXP2_SCALE = math.log2(math.e) / math.sqrt(HEAD_DIM)
MESH = pl.DeviceIdType.MESH
NEAR_FIRST = (1, 7, 2, 6, 3, 5, 4)


def swapped(value, axis, bit):
    mask = 2**bit
    pairs = [(source, source ^ mask) for source in range(lax.axis_size(axis))]
    return lax.ppermute(value, axis, pairs)


def remote(src, dst, send, recv, seq):
    return pltpu.make_async_remote_copy(
        src_ref=src,
        dst_ref=dst,
        send_sem=send,
        recv_sem=recv,
        device_id={"seq": seq},
        device_id_type=MESH,
    )


def attend_tile(query, kv, best, total, accum):
    keys = kv[:, 128:256, :].reshape(8 * GROUP, HEAD_DIM)
    scores = lax.dot_general(
        query, keys, (((1,), (1,)), ((), ())), preferred_element_type=jnp.float32
    )
    pieces = []
    for i in range(8):
        bias = kv[i, 384:400, :].astype(jnp.float32)[0:1]
        pieces.append(scores[:, i * GROUP : (i + 1) * GROUP] + bias)
    peak = functools.reduce(jnp.maximum, pieces)
    new_best = jnp.maximum(best, jnp.max(peak, axis=1, keepdims=True))
    probs = [jnp.exp2((piece - new_best) * EXP2_SCALE) for piece in pieces]
    fade = jnp.exp2((best - new_best) * EXP2_SCALE)
    total = total * fade + functools.reduce(jnp.add, probs)
    weights = jnp.concatenate([prob.astype(jnp.bfloat16) for prob in probs], axis=1)
    values = kv[:, 256:384, :].reshape(8 * GROUP, HEAD_DIM)
    accum = accum * fade + jnp.dot(weights, values, preferred_element_type=jnp.float32)
    return new_best, total, accum


def attention_kernel(
    perm_ref,
    q_ref,
    k_ref,
    v_ref,
    bias_ref,
    att_ref,
    stage,
    buf,
    kv9,
    q9,
    part_out,
    part_in,
    best_s,
    total_s,
    accum_s,
    out_stage,
    zsend,
    zrecv,
    rsend,
    rrecv,
    ysend,
    yrecv,
    qsend,
    qrecv,
    psend,
    precv,
    osend,
    orecv,
):
    me = lax.axis_index("seq")
    y, z = me // Z, me % Z
    right = ((y + 1) % Y) * Z + z
    left = ((y + 3) % Y) * Z + z
    across = ((y + 2) % Y) * Z + z

    def along(t):
        return y * Z + (z + t) % Z

    barrier = pltpu.get_barrier_semaphore()
    for t in range(1, Z):
        pl.semaphore_signal(barrier, inc=1, device_id={"seq": along(t)}, device_id_type=MESH)
    for peer in (right, left, across):
        pl.semaphore_signal(barrier, inc=1, device_id={"seq": peer}, device_id_type=MESH)

    for which, ref in enumerate((q_ref, k_ref, v_ref)):
        rows = jnp.dot(perm_ref[...], ref[...], preferred_element_type=jnp.float32)
        rows = rows.astype(jnp.bfloat16)
        for h in range(HEADS_HERE):
            for c in range(CLIPS):
                stage[3 * h + c, which * 128 : which * 128 + 128, :] = rows[
                    c * 128 : c * 128 + 128, h * 128 : h * 128 + 128
                ]
    for h in range(HEADS_HERE):
        for c in range(CLIPS):
            stage[3 * h + c, 384:400, :] = bias_ref[c]

    pl.semaphore_wait(barrier, Z - 1 + 3)

    sends = []
    for t in NEAR_FIRST:
        copy = remote(
            stage.at[(z + t) % Z], buf.at[0, t], zsend.at[t], zrecv.at[t], along(t)
        )
        copy.start()
        sends.append(copy)
    ring = {
        1: remote(stage.at[8, KV], kv9.at[1, KV], rsend.at[1], rrecv.at[1], along(1)),
        7: remote(stage.at[8, KV], kv9.at[7, KV], rsend.at[7], rrecv.at[7], along(7)),
    }
    for copy in ring.values():
        copy.start()
    for j, peer in ((1, right), (2, left), (3, across)):
        copy = remote(stage.at[8, pl.ds(0, 128)], q9.at[j], qsend.at[j], qrecv.at[j], peer)
        copy.start()
        sends.append(copy)

    def pass_on(t):
        for j, peer in ((1, right), (2, left)):
            copy = remote(
                buf.at[0, t, KV], buf.at[j, t, KV], ysend.at[j - 1, t], yrecv.at[j - 1, t], peer
            )
            copy.start()
            sends.append(copy)

    buf[0, 0] = stage[z]
    pass_on(0)
    kv9[0] = stage[8]
    q9[0] = stage[8, 0:128, :]
    best_s[...] = jnp.full_like(best_s, NEG_FILL)
    total_s[...] = jnp.zeros_like(total_s)
    accum_s[...] = jnp.zeros_like(accum_s)

    def relay(t, onto, peer):
        ring[t].wait_recv()
        ring[onto] = remote(
            kv9.at[t, KV], kv9.at[onto, KV], rsend.at[onto], rrecv.at[onto], peer
        )
        ring[onto].start()

    for i, t in enumerate(NEAR_FIRST):
        sends[i].wait_recv()
        pass_on(t)
        if i == 1:
            relay(1, 2, along(1))
            relay(7, 6, along(7))
        if i == 3:
            relay(2, 3, along(1))
            relay(6, 5, along(7))
        if i == 5:
            relay(3, 4, along(1))
    ring[5].wait_recv()
    ring[4].wait_recv()
    for j in (1, 2, 3):
        sends[6 + j].wait_recv()

    def ninth(tile, carry):
        query = q9[pl.ds(2 * tile, 2)].reshape(256, HEAD_DIM)
        zero = jnp.zeros((256, HEAD_DIM), jnp.float32)
        best, total, accum = attend_tile(query, kv9, zero + NEG_FILL, zero, zero)
        total = jnp.sum(total, axis=1, keepdims=True)
        lane = lax.broadcasted_iota(jnp.int32, (256, HEAD_DIM), 1)
        stats = jnp.where(lane < 64, best, total)
        part_out[pl.ds(2 * tile, 2), :, 0:128] = accum.reshape(2, 128, 128)
        part_out[pl.ds(2 * tile, 2), :, 128:256] = stats.reshape(2, 128, 128)
        return carry

    lax.fori_loop(0, 2, ninth, 0)
    parts = []
    for j, onto, peer in ((1, 2, left), (2, 1, right), (3, 3, across)):
        copy = remote(part_out.at[j], part_in.at[onto], psend.at[j], precv.at[onto], peer)
        copy.start()
        parts.append(copy)

    def out_block(problem):
        row = pl.multiple_of((problem % 3) * 128, 128)
        column = pl.multiple_of((problem // 3) * 128, 128)
        return att_ref.at[pl.ds(row, 128), pl.ds(column, 128)]

    def group(j, carry):
        @pl.when(j == 1)
        def _():
            for t in range(Z):
                for side, peer in ((0, right), (1, left)):
                    remote(
                        buf.at[0, t, KV], buf.at[1 + side, t, KV],
                        ysend.at[side, t], yrecv.at[side, t], peer,
                    ).wait_recv()
                    if t % 2 == side:
                        remote(
                            buf.at[1 + side, t, KV], buf.at[3, t, KV],
                            ysend.at[2, t], yrecv.at[2, t], peer,
                        ).start()

        @pl.when(j == 3)
        def _():
            for t in range(Z):
                remote(
                    buf.at[1 + t % 2, t, KV], buf.at[3, t, KV],
                    ysend.at[2, t], yrecv.at[2, t], (right, left)[t % 2],
                ).wait()

        def one(tile, inner):
            rows = pl.ds(pl.multiple_of(tile * 256, 256), 256)
            query = buf[0, pl.ds(2 * tile, 2), 0:128, :].reshape(256, HEAD_DIM)
            best, total, accum = attend_tile(
                query, buf.at[j], best_s[rows, :], total_s[rows, :], accum_s[rows, :]
            )
            best_s[rows, :] = best
            total_s[rows, :] = total
            accum_s[rows, :] = accum

            @pl.when(j == 3)
            def _():
                result = accum / jnp.sum(total, axis=1, keepdims=True)
                out_stage[pl.ds(2 * tile, 2)] = result.astype(jnp.bfloat16).reshape(2, 128, 128)

                @pl.when(tile == 0)
                def _():
                    pltpu.make_async_copy(out_stage.at[0], out_block(z), osend.at[0]).start()

                @pl.when(tile > 0)
                def _():
                    t = 2 * tile
                    remote(
                        out_stage.at[t], out_block(z), osend.at[t], orecv.at[t],
                        y * Z + (z + Z - t) % Z,
                    ).start()

                t = 2 * tile + 1
                remote(
                    out_stage.at[t], out_block(z), osend.at[t], orecv.at[t],
                    y * Z + (z + Z - t) % Z,
                ).start()

            return inner

        return lax.fori_loop(0, 4, one, carry)

    lax.fori_loop(0, 4, group, 0)

    for copy in parts:
        copy.wait()
    pieces = [part_out.at[0], part_in.at[1], part_in.at[2], part_in.at[3]]
    bests = [piece[:, 128:129] for piece in pieces]
    top = functools.reduce(jnp.maximum, bests)
    weights = [jnp.exp2((best - top) * EXP2_SCALE) for best in bests]
    total = functools.reduce(
        jnp.add, [weight * piece[:, 192:193] for weight, piece in zip(weights, pieces)]
    )
    accum = functools.reduce(
        jnp.add, [weight * piece[:, 0:128] for weight, piece in zip(weights, pieces)]
    )
    att_ref[256:384, 256:384] = (accum / total).astype(jnp.bfloat16)

    pltpu.make_async_copy(out_stage.at[0], out_block(z), osend.at[0]).wait()
    for t in range(1, Z):
        copy = remote(
            out_stage.at[t], out_block((z + t) % Z), osend.at[t], orecv.at[t], along(Z - t)
        )
        copy.wait()
    for copy in sends:
        copy.wait_send()
    for copy in ring.values():
        copy.wait_send()


def attention(perm, queries, keys, values, bias):
    dma = pltpu.SemaphoreType.DMA
    vmem = pltpu.VMEM
    return pl.pallas_call(
        attention_kernel,
        out_shape=jax.ShapeDtypeStruct((384, 384), jnp.bfloat16),
        in_specs=[pl.BlockSpec(memory_space=vmem)] * 5,
        out_specs=pl.BlockSpec(memory_space=vmem),
        scratch_shapes=[
            vmem((9, MSG, 128), jnp.bfloat16),
            vmem((4, Z, MSG, 128), jnp.bfloat16),
            vmem((Z, MSG, 128), jnp.bfloat16),
            vmem((4, 128, 128), jnp.bfloat16),
            vmem((4, 128, 256), jnp.float32),
            vmem((4, 128, 256), jnp.float32),
            vmem((1024, 128), jnp.float32),
            vmem((1024, 128), jnp.float32),
            vmem((1024, 128), jnp.float32),
            vmem((Z, 128, 128), jnp.bfloat16),
            dma((Z,)),
            dma((Z,)),
            dma((Z,)),
            dma((Z,)),
            dma((3, Z)),
            dma((3, Z)),
            dma((4,)),
            dma((4,)),
            dma((4,)),
            dma((4,)),
            dma((Z,)),
            dma((Z,)),
        ],
        compiler_params=pltpu.CompilerParams(
            collective_id=0, has_side_effects=True, vmem_limit_bytes=40 * 2**20
        ),
        name="clip_attention",
    )(perm, queries, keys, values, bias)


def clip_order(slot_clip):
    slots = slot_clip.shape[0]
    first = slot_clip[0]
    live_count = jnp.sum((slot_clip < CLIPS).astype(jnp.int32))
    row = jnp.arange(slots, dtype=jnp.int32)
    clip, rank = row // GROUP, row % GROUP
    slot_of = 3 * rank + (clip + 6 - first) % 3
    return slot_of, slot_of < live_count


def shards(
    queries, keys, values, residual, w_out, w_up, w_down, modulation, guide_scale, slot_clip, owner
):
    slots = slot_clip.shape[0]
    slot_of, live = clip_order(slot_clip)
    perm = (slot_of[:, None] == jnp.arange(slots, dtype=jnp.int32)[None, :]).astype(jnp.bfloat16)
    bias = jnp.broadcast_to(
        jnp.where(live, 0.0, NEG_FILL).astype(jnp.bfloat16).reshape(CLIPS, 1, GROUP),
        (CLIPS, 16, GROUP),
    )
    attended = attention(perm, queries[0], keys[0], values[0], bias)
    partial_out = jnp.dot(attended, w_out, preferred_element_type=jnp.float32)
    mod = jnp.repeat(modulation, GROUP, axis=0)
    columns = D // lax.axis_size("blk")
    col_start = lax.axis_index("blk") * columns
    gate_mlp = lax.dynamic_slice_in_dim(mod[:, 3], col_start, columns, 1)
    stream = jnp.dot(perm, residual[0], preferred_element_type=jnp.float32)
    projected = lax.psum(partial_out.astype(jnp.bfloat16), "blk").astype(jnp.float32)
    mixed = stream + mod[:, 0] * projected
    centre = mixed - jnp.mean(mixed, axis=-1, keepdims=True)
    spread = jnp.mean(centre * centre, axis=-1, keepdims=True)
    normed = (centre * lax.rsqrt(spread + 1e-06) * (1.0 + mod[:, 2]) + mod[:, 1]).astype(
        jnp.bfloat16
    )
    mixed_cols = lax.dynamic_slice_in_dim(mixed, col_start, columns, 1)
    hidden = jax.nn.gelu(
        jnp.dot(normed, w_up, preferred_element_type=jnp.float32), approximate=True
    ).astype(jnp.bfloat16)
    terms = jnp.dot(hidden, w_down, preferred_element_type=jnp.float32)
    summed = lax.psum_scatter(
        terms.astype(jnp.bfloat16), "blk", scatter_dimension=1, tiled=True
    ).astype(jnp.float32)
    block_out = (mixed_cols + gate_mlp * summed).astype(jnp.bfloat16)

    side = lax.axis_index("cfg")
    half_group = GROUP // 2
    split = block_out.reshape(CLIPS, 2, half_group, columns)
    mine = lax.dynamic_index_in_dim(split, side, 1, keepdims=False)
    partner = swapped(lax.dynamic_index_in_dim(split, 1 - side, 1, keepdims=False), "cfg", 0)
    cond = jnp.where(side == 0, mine, partner).astype(jnp.float32)
    uncond = jnp.where(side == 0, partner, mine).astype(jnp.float32)
    guided = uncond + guide_scale[:, None, None] * (cond - uncond)
    live_half = lax.dynamic_index_in_dim(live.reshape(CLIPS, 2, half_group), side, 1, keepdims=False)
    guided = jnp.where(live_half[:, :, None], guided, 0.0).astype(jnp.bfloat16)
    guided = guided.reshape(slots // 2, columns)

    seq_count = lax.axis_size("seq")
    capacity = max(2, slots // seq_count)
    half_len = slots // 2
    owner_half = lax.dynamic_slice_in_dim(owner[:, 0], side * half_len, half_len, 0)
    place = jnp.arange(half_len, dtype=jnp.int32)
    earlier = (owner_half[:, None] == owner_half[None, :]) & (place[None, :] < place[:, None])
    rank = jnp.sum(earlier.astype(jnp.int32), axis=1)
    target = owner_half * capacity + rank
    slot_half = lax.dynamic_index_in_dim(
        slot_of.reshape(CLIPS, 2, half_group), side, 1, keepdims=False
    ).reshape(half_len) - side * half_len
    target = jnp.sum(
        jnp.where(slot_half[:, None] == place[None, :], target[None, :], 0), axis=1
    )
    placing = (
        jnp.arange(seq_count * capacity, dtype=jnp.int32)[:, None] == target[None, :]
    ).astype(jnp.bfloat16)
    outgoing = jnp.dot(placing, guided, preferred_element_type=jnp.float32).astype(jnp.bfloat16)
    outgoing = outgoing.reshape(seq_count, capacity, columns)
    arrived = lax.all_to_all(outgoing, "seq", split_axis=0, concat_axis=0, tiled=True)
    return arrived.reshape(1, seq_count * capacity, columns)


def solution(mesh):
    placed = (
        P("cfg", "seq", "blk"),
        P("cfg", "seq", "blk"),
        P("cfg", "seq", "blk"),
        P("cfg", "seq", None),
        P("blk", None),
        P(None, "blk"),
        P("blk", None),
        P(),
        P(),
        P("seq"),
        P("seq", None),
    )
    return jax.shard_map(
        shards, mesh=mesh, in_specs=placed, out_specs=P("cfg", "seq", "blk"), check_vma=False
    )
```

```python
import functools
import math

import jax
import jax.numpy as jnp
from jax import lax
from jax.experimental import pallas as pl
from jax.experimental.pallas import tpu as pltpu
from jax.sharding import PartitionSpec as P

D = 1536
HEAD_DIM = 128
CLIPS = 3
HEADS_HERE = 3
GROUP = 128
Y, Z = 4, 8
MSG = 400
KV = pl.ds(128, 272)
NEG_FILL = -1e30
EXP2_SCALE = math.log2(math.e) / math.sqrt(HEAD_DIM)
MESH = pl.DeviceIdType.MESH
NEAR_FIRST = (1, 7, 2, 6, 3, 5, 4)
X = 4
SLOTS = 384
HALF = 192
CAP = 12
TOP, LOW = pl.ds(0, HALF), pl.ds(HALF, HALF)


def remote(src, dst, send, recv, peer):
    return pltpu.make_async_remote_copy(
        src_ref=src,
        dst_ref=dst,
        send_sem=send,
        recv_sem=recv,
        device_id=peer,
        device_id_type=MESH,
    )


def attend_tile(query, kv, best, total, accum):
    keys = kv[:, 128:256, :].reshape(8 * GROUP, HEAD_DIM)
    scores = lax.dot_general(
        query, keys, (((1,), (1,)), ((), ())), preferred_element_type=jnp.float32
    )
    pieces = []
    for i in range(8):
        bias = kv[i, 384:400, :].astype(jnp.float32)[0:1]
        pieces.append(scores[:, i * GROUP : (i + 1) * GROUP] + bias)
    peak = functools.reduce(jnp.maximum, pieces)
    new_best = jnp.maximum(best, jnp.max(peak, axis=1, keepdims=True))
    probs = [jnp.exp2((piece - new_best) * EXP2_SCALE) for piece in pieces]
    fade = jnp.exp2((best - new_best) * EXP2_SCALE)
    total = total * fade + functools.reduce(jnp.add, probs)
    weights = jnp.concatenate([prob.astype(jnp.bfloat16) for prob in probs], axis=1)
    values = kv[:, 256:384, :].reshape(8 * GROUP, HEAD_DIM)
    accum = accum * fade + jnp.dot(weights, values, preferred_element_type=jnp.float32)
    return new_best, total, accum


def block_kernel(
    clip_ref,
    owner_ref,
    guide_ref,
    q_hbm,
    k_hbm,
    v_hbm,
    res_hbm,
    mod_hbm,
    w_out_hbm,
    w_up_hbm,
    w_down_hbm,
    out_ref,
    qkv,
    perm,
    stage,
    buf,
    kv9,
    q9,
    part_out,
    part_in,
    best_s,
    total_s,
    accum_s,
    out_stage,
    att,
    w_out,
    w_up,
    w_down,
    residual,
    mod,
    mixed,
    normed,
    hidden,
    far,
    near,
    transit,
    final,
    mine,
    theirs,
    placing,
    repack,
    going,
    landed,
    turned,
    lsem,
    zsend,
    zrecv,
    rsend,
    rrecv,
    ysend,
    yrecv,
    qsend,
    qrecv,
    psend,
    precv,
    osend,
    orecv,
    wsend,
    wrecv,
    csend,
    crecv,
    asend,
    arecv,
    tsend,
    trecv,
    fsend,
    frecv,
    esend,
    erecv,
    gsend,
    grecv,
    hsend,
    hrecv,
):
    f32, bf16 = jnp.float32, jnp.bfloat16
    me = lax.axis_index("seq")
    side = lax.axis_index("cfg")
    blk = lax.axis_index("blk")
    y, z = me // Z, me % Z

    def up(t):
        return {"seq": ((y + t) % Y) * Z + z}

    def along(t):
        return {"seq": y * Z + (z + t) % Z}

    def over(t):
        return {"blk": (blk + t) % X}

    right, left, across = up(1), up(3), up(2)
    other_core = {"cfg": 1 - side}

    barrier = pltpu.get_barrier_semaphore()
    peers = [along(t) for t in range(1, Z)] + [up(t) for t in range(1, Y)]
    peers += [over(t) for t in range(1, X)] + [other_core]
    for peer in peers:
        pl.semaphore_signal(barrier, inc=1, device_id=peer, device_id_type=MESH)

    loads = [
        pltpu.make_async_copy(src, dst, lsem.at[i])
        for i, (src, dst) in enumerate(
            (
                (q_hbm.at[0], qkv.at[0]),
                (k_hbm.at[0], qkv.at[1]),
                (v_hbm.at[0], qkv.at[2]),
                (res_hbm.at[0], residual),
                (mod_hbm, mod),
                (w_out_hbm, w_out.at[0]),
                (w_up_hbm, w_up),
                (w_down_hbm, w_down),
            )
        )
    ]
    for copy in loads:
        copy.start()

    clips = clip_ref[...].astype(f32)
    first = clips[0:1, 0:1]
    count = jnp.sum(jnp.where(clips < CLIPS, 1.0, 0.0), axis=1, keepdims=True)
    row = lax.broadcasted_iota(jnp.int32, (SLOTS, SLOTS), 0).astype(f32)
    lane = lax.broadcasted_iota(jnp.int32, (SLOTS, SLOTS), 1).astype(f32)
    row_clip = jnp.where(row >= 128, 1.0, 0.0) + jnp.where(row >= 256, 1.0, 0.0)
    step = row_clip - first
    step = jnp.where(step < 0, step + 3, step)
    perm[...] = jnp.where(3 * (row - 128 * row_clip) + step == lane, 1.0, 0.0).astype(bf16)
    rank = lax.broadcasted_iota(jnp.int32, (16, 128), 1).astype(f32)
    for c in range(CLIPS):
        step = c - first
        step = jnp.where(step < 0, step + 3, step)
        bias = jnp.where(3 * rank + step < count, 0.0, NEG_FILL).astype(bf16)
        for h in range(HEADS_HERE):
            stage[3 * h + c, 384:400, :] = bias

    for which in range(3):
        loads[which].wait()
        rows = jnp.dot(perm[...], qkv[which], preferred_element_type=f32).astype(bf16)
        for h in range(HEADS_HERE):
            for c in range(CLIPS):
                stage[3 * h + c, which * 128 : which * 128 + 128, :] = rows[
                    c * 128 : c * 128 + 128, h * 128 : h * 128 + 128
                ]

    pl.semaphore_wait(barrier, len(peers))

    sends = []
    for t in NEAR_FIRST:
        copy = remote(
            stage.at[(z + t) % Z], buf.at[0, t], zsend.at[t], zrecv.at[t], along(t)
        )
        copy.start()
        sends.append(copy)
    ring = {
        1: remote(stage.at[8, KV], kv9.at[1, KV], rsend.at[1], rrecv.at[1], along(1)),
        7: remote(stage.at[8, KV], kv9.at[7, KV], rsend.at[7], rrecv.at[7], along(7)),
    }
    for copy in ring.values():
        copy.start()
    for j, peer in ((1, right), (2, left), (3, across)):
        copy = remote(stage.at[8, pl.ds(0, 128)], q9.at[j], qsend.at[j], qrecv.at[j], peer)
        copy.start()
        sends.append(copy)

    def pass_on(t):
        for j, peer in ((1, right), (2, left)):
            copy = remote(
                buf.at[0, t, KV], buf.at[j, t, KV], ysend.at[j - 1, t], yrecv.at[j - 1, t], peer
            )
            copy.start()
            sends.append(copy)

    buf[0, 0] = stage[z]
    pass_on(0)

    own_rows = pl.ds(pl.multiple_of(side * HALF, HALF), HALF)
    shares = []
    for j, t in ((1, 1), (2, 3), (3, 2)):
        copy = remote(
            w_out_hbm.at[own_rows], w_out.at[j, own_rows], wsend.at[j], wrecv.at[j], over(t)
        )
        copy.start()
        shares.append(copy)

    kv9[0] = stage[8]
    q9[0] = stage[8, 0:128, :]
    best_s[...] = jnp.full_like(best_s, NEG_FILL)
    total_s[...] = jnp.zeros_like(total_s)
    accum_s[...] = jnp.zeros_like(accum_s)

    owners = owner_ref[...].astype(f32)
    owner_column = jnp.sum(jnp.where(row == lane, owners, 0.0), axis=1, keepdims=True)
    half_start = jnp.where(lane >= HALF, float(HALF), 0.0)
    earlier = (owner_column == owners) & (row < lane) & (row >= half_start)
    ranks = jnp.sum(jnp.where(earlier, 1.0, 0.0), axis=0, keepdims=True)
    owner_y = functools.reduce(
        jnp.add, [jnp.where(owners >= edge, 1.0, 0.0) for edge in (8, 16, 24)]
    )
    target = (owners - 8 * owner_y) * 48 + owner_y * CAP + ranks
    low = side.astype(f32) * HALF
    slot = lane[0:1]
    chosen = (slot < count) & (slot >= low) & (slot < low + HALF)
    target = jnp.where(chosen, target, -1.0)
    by_slot = jnp.where(row == target, 1.0, 0.0).astype(bf16)
    half_perm = jnp.concatenate(
        [perm[pl.ds(pl.multiple_of(c * 128 + side * 64, 64), 64), :] for c in range(CLIPS)], axis=0
    )
    placing[...] = lax.dot_general(
        by_slot, half_perm, (((1,), (1,)), ((), ())), preferred_element_type=f32
    ).astype(bf16)
    from_z = jnp.floor((slot + 0.5) * (1.0 / 48.0))
    within = slot - 48 * from_z
    to_y = jnp.floor((within + 0.5) * (1.0 / CAP))
    repack[...] = jnp.where(
        row == to_y * 96 + from_z * CAP + within - CAP * to_y, 1.0, 0.0
    ).astype(bf16)

    loads[3].wait()
    for k in range(3):
        cols = slice(512 * k, 512 * k + 512)
        mixed[:, cols] = jnp.dot(perm[...], residual[:, cols], preferred_element_type=f32)

    def relay(t, onto, peer):
        ring[t].wait_recv()
        ring[onto] = remote(
            kv9.at[t, KV], kv9.at[onto, KV], rsend.at[onto], rrecv.at[onto], peer
        )
        ring[onto].start()

    for i, t in enumerate(NEAR_FIRST):
        sends[i].wait_recv()
        pass_on(t)
        if i == 1:
            relay(1, 2, along(1))
            relay(7, 6, along(7))
        if i == 3:
            relay(2, 3, along(1))
            relay(6, 5, along(7))
        if i == 5:
            relay(3, 4, along(1))
    ring[5].wait_recv()
    ring[4].wait_recv()
    for j in (1, 2, 3):
        sends[6 + j].wait_recv()

    def ninth(tile, carry):
        query = q9[pl.ds(2 * tile, 2)].reshape(256, HEAD_DIM)
        zero = jnp.zeros((256, HEAD_DIM), f32)
        best, total, accum = attend_tile(query, kv9, zero + NEG_FILL, zero, zero)
        total = jnp.sum(total, axis=1, keepdims=True)
        lane = lax.broadcasted_iota(jnp.int32, (256, HEAD_DIM), 1)
        stats = jnp.where(lane < 64, best, total)
        part_out[pl.ds(2 * tile, 2), :, 0:128] = accum.reshape(2, 128, 128)
        part_out[pl.ds(2 * tile, 2), :, 128:256] = stats.reshape(2, 128, 128)
        return carry

    lax.fori_loop(0, 2, ninth, 0)
    parts = []
    for j, onto, peer in ((1, 2, left), (2, 1, right), (3, 3, across)):
        copy = remote(part_out.at[j], part_in.at[onto], psend.at[j], precv.at[onto], peer)
        copy.start()
        parts.append(copy)

    def out_block(problem):
        row = pl.multiple_of((problem % 3) * 128, 128)
        column = pl.multiple_of((problem // 3) * 128, 128)
        return att.at[0, pl.ds(row, 128), pl.ds(column, 128)]

    def group(j, carry):
        @pl.when(j == 1)
        def _():
            for t in range(Z):
                for way, peer in ((0, right), (1, left)):
                    remote(
                        buf.at[0, t, KV], buf.at[1 + way, t, KV],
                        ysend.at[way, t], yrecv.at[way, t], peer,
                    ).wait_recv()
                    if t % 2 == way:
                        remote(
                            buf.at[1 + way, t, KV], buf.at[3, t, KV],
                            ysend.at[2, t], yrecv.at[2, t], peer,
                        ).start()

        @pl.when(j == 3)
        def _():
            for t in range(Z):
                remote(
                    buf.at[1 + t % 2, t, KV], buf.at[3, t, KV],
                    ysend.at[2, t], yrecv.at[2, t], (right, left)[t % 2],
                ).wait()

        def one(tile, inner):
            rows = pl.ds(pl.multiple_of(tile * 256, 256), 256)
            query = buf[0, pl.ds(2 * tile, 2), 0:128, :].reshape(256, HEAD_DIM)
            best, total, accum = attend_tile(
                query, buf.at[j], best_s[rows, :], total_s[rows, :], accum_s[rows, :]
            )
            best_s[rows, :] = best
            total_s[rows, :] = total
            accum_s[rows, :] = accum

            @pl.when(j == 3)
            def _():
                result = accum / jnp.sum(total, axis=1, keepdims=True)
                out_stage[pl.ds(2 * tile, 2)] = result.astype(bf16).reshape(2, 128, 128)

                @pl.when(tile == 0)
                def _():
                    pltpu.make_async_copy(out_stage.at[0], out_block(z), osend.at[0]).start()

                @pl.when(tile > 0)
                def _():
                    t = 2 * tile
                    remote(
                        out_stage.at[t], out_block(z), osend.at[t], orecv.at[t], along(Z - t)
                    ).start()

                t = 2 * tile + 1
                remote(
                    out_stage.at[t], out_block(z), osend.at[t], orecv.at[t], along(Z - t)
                ).start()

            return inner

        return lax.fori_loop(0, 4, one, carry)

    lax.fori_loop(0, 4, group, 0)

    swaps = []
    for j, copy in enumerate(shares, 1):
        copy.wait()
        swap = remote(
            w_out.at[j, own_rows], w_out.at[j, own_rows], csend.at[j], crecv.at[j], other_core
        )
        swap.start()
        swaps.append(swap)

    for copy in parts:
        copy.wait()
    pieces = [part_out.at[0], part_in.at[1], part_in.at[2], part_in.at[3]]
    bests = [piece[:, 128:129] for piece in pieces]
    top = functools.reduce(jnp.maximum, bests)
    weights = [jnp.exp2((best - top) * EXP2_SCALE) for best in bests]
    total = functools.reduce(
        jnp.add, [weight * piece[:, 192:193] for weight, piece in zip(weights, pieces)]
    )
    accum = functools.reduce(
        jnp.add, [weight * piece[:, 0:128] for weight, piece in zip(weights, pieces)]
    )
    att[0, 256:384, 256:384] = (accum / total).astype(bf16)

    pltpu.make_async_copy(out_stage.at[0], out_block(z), osend.at[0]).wait()
    for t in range(1, Z):
        remote(
            out_stage.at[t], out_block((z + t) % Z), osend.at[t], orecv.at[t], along(Z - t)
        ).wait_recv()

    gathers = {}

    def hop(src, slot, part, peer):
        rows = (TOP, LOW)[part]
        copy = remote(
            att.at[src, rows], att.at[slot, rows], asend.at[slot, part], arecv.at[slot, part], peer
        )
        copy.start()
        gathers[slot, part] = copy

    hop(0, 1, 0, over(1))
    hop(0, 2, 1, over(3))
    hop(0, 1, 1, over(1))
    hop(0, 2, 0, over(3))

    for copy in loads[4:6]:
        copy.wait()
    for copy in swaps:
        copy.wait()

    def project(slot):
        rows = att[slot]

        def one(k, carry):
            cols = pl.ds(pl.multiple_of(k * 512, 512), 512)
            term = jnp.dot(rows, w_out[slot, :, cols], preferred_element_type=f32)
            for c in range(CLIPS):
                part = slice(128 * c, 128 * c + 128)
                mixed[part, cols] += mod[c, 0:1, cols] * term[part]
            return carry

        lax.fori_loop(0, 3, one, 0)

    gathers[1, 0].wait_recv()
    hop(1, 3, 0, over(1))
    gathers[2, 1].wait_recv()
    hop(2, 3, 1, over(3))
    project(0)
    gathers[1, 1].wait_recv()
    project(1)
    gathers[2, 0].wait_recv()
    project(2)
    gathers[3, 0].wait_recv()
    gathers[3, 1].wait_recv()
    project(3)

    def normalise(k, carry):
        for c in range(CLIPS):
            rows = pl.ds(pl.multiple_of(c * 128 + k * 32, 32), 32)
            value = mixed[rows, :]
            centre = value - jnp.mean(value, axis=1, keepdims=True)
            spread = jnp.mean(centre * centre, axis=1, keepdims=True)
            scaled = centre * lax.rsqrt(spread + 1e-06) * (1.0 + mod[c, 2:3, :]) + mod[c, 1:2, :]
            normed[rows, :] = scaled.astype(bf16)
        return carry

    lax.fori_loop(0, 4, normalise, 0)

    loads[6].wait()

    def expand(k, carry):
        cols = pl.ds(pl.multiple_of(k * 512, 512), 512)
        value = jnp.dot(normed[...], w_up[:, cols], preferred_element_type=f32)
        hidden[:, cols] = jax.nn.gelu(value, approximate=True).astype(bf16)
        return carry

    lax.fori_loop(0, 3, expand, 0)

    loads[7].wait()

    def contract(t):
        cols = pl.ds(pl.multiple_of(((blk + t) % X) * SLOTS, SLOTS), SLOTS)
        return jnp.dot(hidden[...], w_down[:, cols], preferred_element_type=f32)

    far[...] = contract(2).astype(bf16)
    passing = [
        remote(far.at[TOP], transit.at[0], tsend.at[0], trecv.at[0], over(1)),
        remote(far.at[LOW], transit.at[1], tsend.at[1], trecv.at[1], over(3)),
    ]
    for copy in passing:
        copy.start()
    finals = [
        remote(near.at[0, TOP], final.at[0], fsend.at[0], frecv.at[0], over(1)),
        remote(near.at[0, LOW], final.at[1], fsend.at[1], frecv.at[1], over(1)),
        remote(near.at[1, TOP], final.at[2], fsend.at[2], frecv.at[2], over(3)),
        remote(near.at[1, LOW], final.at[3], fsend.at[3], frecv.at[3], over(3)),
    ]
    to_right = contract(1)
    near[0, HALF:] = to_right[HALF:].astype(bf16)
    finals[1].start()
    to_left = contract(3)
    near[1, :HALF] = to_left[:HALF].astype(bf16)
    finals[2].start()
    passing[0].wait_recv()
    near[0, :HALF] = (to_right[:HALF] + transit[0].astype(f32)).astype(bf16)
    finals[0].start()
    passing[1].wait_recv()
    near[1, HALF:] = (to_left[HALF:] + transit[1].astype(f32)).astype(bf16)
    finals[3].start()
    own = contract(0)
    for copy in finals:
        copy.wait_recv()
    own_cols = pl.ds(pl.multiple_of(blk * SLOTS, SLOTS), SLOTS)
    for c in range(CLIPS):
        for half in range(2):
            start = c * 128 + half * 64
            which, rows = start // HALF, slice(start % HALF, start % HALF + 64)
            summed = own[start : start + 64] + final[which, rows].astype(f32)
            summed = summed + final[2 + which, rows].astype(f32)
            value = mixed[start : start + 64, own_cols] + mod[c, 3:4, own_cols] * summed
            mine[half, c * 64 : c * 64 + 64] = value.astype(bf16)

    exchange = remote(mine.at[1 - side], theirs, esend.at[0], erecv.at[0], other_core)
    exchange.start()
    exchange.wait_recv()
    ours, others = mine[side].astype(f32), theirs[...].astype(f32)
    conditional = jnp.where(side == 0, ours, others)
    plain = jnp.where(side == 0, others, ours)
    guided = jnp.concatenate(
        [
            plain[64 * c : 64 * c + 64]
            + guide_ref[c] * (conditional[64 * c : 64 * c + 64] - plain[64 * c : 64 * c + 64])
            for c in range(CLIPS)
        ],
        axis=0,
    ).astype(bf16)

    here = pl.ds(pl.multiple_of(z * 48, 16), 48)
    trips, last = [], []
    for k in range(3):
        going[k] = jnp.dot(
            placing[...], guided[:, 128 * k : 128 * k + 128], preferred_element_type=f32
        ).astype(bf16)
        for t in NEAR_FIRST:
            there = pl.ds(pl.multiple_of(((z + t) % Z) * 48, 16), 48)
            copy = remote(
                going.at[k, there], landed.at[k, here], gsend.at[k, t], grecv.at[k, t], along(t)
            )
            copy.start()
            trips.append(copy)
        landed[k, here, :] = going[k, here, :]
    row_here = pl.ds(pl.multiple_of(y * 96, 96), 96)
    for k in range(3):
        cols = pl.ds(128 * k, 128)
        for copy in trips[7 * k : 7 * k + 7]:
            copy.wait_recv()
        turned[k] = jnp.dot(repack[...], landed[k], preferred_element_type=f32).astype(bf16)
        for t in (1, 3, 2):
            there = pl.ds(pl.multiple_of(((y + t) % Y) * 96, 96), 96)
            copy = remote(
                turned.at[k, there], out_ref.at[0, row_here, cols],
                hsend.at[k, t], hrecv.at[k, t], up(t),
            )
            copy.start()
            last.append(copy)
        out_ref[0, row_here, 128 * k : 128 * k + 128] = turned[k, row_here, :]
    for copy in last:
        copy.wait()

    for t in range(1, Z):
        remote(
            out_stage.at[t], out_block((z + t) % Z), osend.at[t], orecv.at[t], along(Z - t)
        ).wait_send()
    for copy in [*sends, *ring.values(), *gathers.values(), *passing, *finals, exchange, *trips]:
        copy.wait_send()


def block(clips, owners, guide_scale, *arrays):
    dma = pltpu.SemaphoreType.DMA
    vmem = pltpu.VMEM
    f32, bf16 = jnp.float32, jnp.bfloat16
    return pl.pallas_call(
        block_kernel,
        out_shape=jax.ShapeDtypeStruct((1, SLOTS, SLOTS), bf16),
        in_specs=[
            pl.BlockSpec(memory_space=vmem),
            pl.BlockSpec(memory_space=vmem),
            pl.BlockSpec(memory_space=pltpu.SMEM),
            *[pl.BlockSpec(memory_space=pl.ANY)] * 8,
        ],
        out_specs=pl.BlockSpec(memory_space=vmem),
        scratch_shapes=[
            vmem((3, SLOTS, SLOTS), bf16),
            vmem((SLOTS, SLOTS), bf16),
            vmem((9, MSG, 128), bf16),
            vmem((4, Z, MSG, 128), bf16),
            vmem((Z, MSG, 128), bf16),
            vmem((4, 128, 128), bf16),
            vmem((4, 128, 256), f32),
            vmem((4, 128, 256), f32),
            vmem((1024, 128), f32),
            vmem((1024, 128), f32),
            vmem((1024, 128), f32),
            vmem((Z, 128, 128), bf16),
            vmem((4, SLOTS, SLOTS), bf16),
            vmem((4, SLOTS, D), bf16),
            vmem((D, D), bf16),
            vmem((D, D), bf16),
            vmem((SLOTS, D), bf16),
            vmem((CLIPS, 4, D), f32),
            vmem((SLOTS, D), f32),
            vmem((SLOTS, D), bf16),
            vmem((SLOTS, D), bf16),
            vmem((SLOTS, SLOTS), bf16),
            vmem((2, SLOTS, SLOTS), bf16),
            vmem((2, HALF, SLOTS), bf16),
            vmem((4, HALF, SLOTS), bf16),
            vmem((2, HALF, SLOTS), bf16),
            vmem((HALF, SLOTS), bf16),
            vmem((SLOTS, HALF), bf16),
            vmem((SLOTS, SLOTS), bf16),
            vmem((3, SLOTS, 128), bf16),
            vmem((3, SLOTS, 128), bf16),
            vmem((3, SLOTS, 128), bf16),
            dma((8,)),
            dma((Z,)),
            dma((Z,)),
            dma((Z,)),
            dma((Z,)),
            dma((3, Z)),
            dma((3, Z)),
            dma((4,)),
            dma((4,)),
            dma((4,)),
            dma((4,)),
            dma((Z,)),
            dma((Z,)),
            dma((4,)),
            dma((4,)),
            dma((4,)),
            dma((4,)),
            dma((4, 2)),
            dma((4, 2)),
            dma((2,)),
            dma((2,)),
            dma((4,)),
            dma((4,)),
            dma((1,)),
            dma((1,)),
            dma((3, Z)),
            dma((3, Z)),
            dma((3, Y)),
            dma((3, Y)),
        ],
        compiler_params=pltpu.CompilerParams(
            collective_id=0, has_side_effects=True, vmem_limit_bytes=56 * 2**20
        ),
        name="guided_block",
    )(clips, owners, guide_scale, *arrays)


def shards(
    queries, keys, values, residual, w_out, w_up, w_down, modulation, guide_scale, slot_clip, owner
):
    return block(
        slot_clip.reshape(1, SLOTS),
        owner.reshape(1, SLOTS),
        guide_scale,
        queries,
        keys,
        values,
        residual,
        modulation,
        w_out,
        w_up,
        w_down,
    )


def solution(mesh):
    placed = (
        P("cfg", "seq", "blk"),
        P("cfg", "seq", "blk"),
        P("cfg", "seq", "blk"),
        P("cfg", "seq", None),
        P("blk", None),
        P(None, "blk"),
        P("blk", None),
        P(),
        P(),
        P("seq"),
        P("seq", None),
    )
    return jax.shard_map(
        shards, mesh=mesh, in_specs=placed, out_specs=P("cfg", "seq", "blk"), check_vma=False
    )
```

```python
import functools
import math

import jax
import jax.numpy as jnp
from jax import lax
from jax.experimental import pallas as pl
from jax.experimental.pallas import tpu as pltpu
from jax.sharding import PartitionSpec as P

D = 1536
HEAD_DIM = 128
CLIPS = 3
HEADS_HERE = 3
GROUP = 128
Y, Z = 4, 8
MSG = 400
KV = pl.ds(128, 272)
NEG_FILL = -1e30
EXP2_SCALE = math.log2(math.e) / math.sqrt(HEAD_DIM)
MESH = pl.DeviceIdType.MESH
NEAR_FIRST = (1, 7, 2, 6, 3, 5, 4)
X = 4
SLOTS = 384
HALF = 192
CAP = 12
TOP, LOW = pl.ds(0, HALF), pl.ds(HALF, HALF)


def remote(src, dst, send, recv, peer):
    return pltpu.make_async_remote_copy(
        src_ref=src,
        dst_ref=dst,
        send_sem=send,
        recv_sem=recv,
        device_id=peer,
        device_id_type=MESH,
    )


def attend_tile(query, kv, best, total, accum):
    count = kv.shape[0]
    keys = kv[:, 128:256, :].reshape(count * GROUP, HEAD_DIM)
    scores = lax.dot_general(
        query, keys, (((1,), (1,)), ((), ())), preferred_element_type=jnp.float32
    )
    pieces = []
    for i in range(count):
        bias = kv[i, 384:400, :].astype(jnp.float32)[0:1]
        pieces.append(scores[:, i * GROUP : (i + 1) * GROUP] + bias)
    peak = functools.reduce(jnp.maximum, pieces)
    new_best = jnp.maximum(best, jnp.max(peak, axis=1, keepdims=True))
    probs = [jnp.exp2((piece - new_best) * EXP2_SCALE) for piece in pieces]
    fade = jnp.exp2((best - new_best) * EXP2_SCALE)
    total = total * fade + functools.reduce(jnp.add, probs)
    weights = jnp.concatenate([prob.astype(jnp.bfloat16) for prob in probs], axis=1)
    values = kv[:, 256:384, :].reshape(count * GROUP, HEAD_DIM)
    accum = accum * fade + jnp.dot(weights, values, preferred_element_type=jnp.float32)
    return new_best, total, accum


def block_kernel(
    clip_ref,
    owner_ref,
    guide_ref,
    q_hbm,
    k_hbm,
    v_hbm,
    res_hbm,
    mod_hbm,
    w_out_hbm,
    w_up_hbm,
    w_down_hbm,
    out_ref,
    qkv,
    perm,
    stage,
    buf,
    kv9,
    q9,
    part_out,
    part_in,
    stat_out,
    stat_in,
    best_s,
    total_s,
    accum_s,
    out_stage,
    att,
    w_out,
    w_up,
    w_down,
    residual,
    mod,
    mixed,
    normed,
    hidden,
    far,
    near,
    ready,
    transit,
    final,
    mine,
    theirs,
    placing,
    repack,
    going,
    landed,
    turned,
    lsem,
    zsend,
    zrecv,
    rsend,
    rrecv,
    ysend,
    yrecv,
    qsend,
    qrecv,
    psend,
    precv,
    ssend,
    srecv,
    osend,
    orecv,
    wsend,
    wrecv,
    csend,
    crecv,
    asend,
    arecv,
    tsend,
    trecv,
    fsend,
    frecv,
    esend,
    erecv,
    gsend,
    grecv,
    hsend,
    hrecv,
):
    f32, bf16 = jnp.float32, jnp.bfloat16
    me = lax.axis_index("seq")
    side = lax.axis_index("cfg")
    blk = lax.axis_index("blk")
    y, z = me // Z, me % Z

    def up(t):
        return {"seq": ((y + t) % Y) * Z + z}

    def along(t):
        return {"seq": y * Z + (z + t) % Z}

    def over(t):
        return {"blk": (blk + t) % X}

    right, left, across = up(1), up(3), up(2)
    other_core = {"cfg": 1 - side}

    barrier = pltpu.get_barrier_semaphore()
    peers = [along(t) for t in range(1, Z)] + [up(t) for t in range(1, Y)]
    peers += [over(t) for t in range(1, X)] + [other_core]
    for peer in peers:
        pl.semaphore_signal(barrier, inc=1, device_id=peer, device_id_type=MESH)

    loads = [
        pltpu.make_async_copy(src, dst, lsem.at[i])
        for i, (src, dst) in enumerate(
            (
                (q_hbm.at[0], qkv.at[0]),
                (k_hbm.at[0], qkv.at[1]),
                (v_hbm.at[0], qkv.at[2]),
                (res_hbm.at[0], residual),
                (mod_hbm, mod),
                (w_out_hbm, w_out.at[0]),
                (w_up_hbm, w_up),
                (w_down_hbm, w_down),
            )
        )
    ]
    for copy in loads:
        copy.start()

    clips = clip_ref[...].astype(f32)
    first = clips[0:1, 0:1]
    count = jnp.sum(jnp.where(clips < CLIPS, 1.0, 0.0), axis=1, keepdims=True)
    row = lax.broadcasted_iota(jnp.int32, (SLOTS, SLOTS), 0).astype(f32)
    lane = lax.broadcasted_iota(jnp.int32, (SLOTS, SLOTS), 1).astype(f32)
    row_clip = jnp.where(row >= 128, 1.0, 0.0) + jnp.where(row >= 256, 1.0, 0.0)
    step = row_clip - first
    step = jnp.where(step < 0, step + 3, step)
    perm[...] = jnp.where(3 * (row - 128 * row_clip) + step == lane, 1.0, 0.0).astype(bf16)
    rank = lax.broadcasted_iota(jnp.int32, (16, 128), 1).astype(f32)
    for c in range(CLIPS):
        step = c - first
        step = jnp.where(step < 0, step + 3, step)
        bias = jnp.where(3 * rank + step < count, 0.0, NEG_FILL).astype(bf16)
        for h in range(HEADS_HERE):
            stage[3 * h + c, 384:400, :] = bias

    for which in range(3):
        loads[which].wait()
        rows = jnp.dot(perm[...], qkv[which], preferred_element_type=f32).astype(bf16)
        for h in range(HEADS_HERE):
            for c in range(CLIPS):
                stage[3 * h + c, which * 128 : which * 128 + 128, :] = rows[
                    c * 128 : c * 128 + 128, h * 128 : h * 128 + 128
                ]

    pl.semaphore_wait(barrier, len(peers))

    ring = {
        1: remote(stage.at[8, KV], kv9.at[1, KV], rsend.at[1], rrecv.at[1], along(1)),
        7: remote(stage.at[8, KV], kv9.at[7, KV], rsend.at[7], rrecv.at[7], along(7)),
    }
    for copy in ring.values():
        copy.start()
    sends = []
    for t in NEAR_FIRST:
        copy = remote(
            stage.at[(z + t) % Z], buf.at[0, t], zsend.at[t], zrecv.at[t], along(t)
        )
        copy.start()
        sends.append(copy)
    for j, peer in ((1, right), (2, left), (3, across)):
        copy = remote(stage.at[8, pl.ds(0, 128)], q9.at[j], qsend.at[j], qrecv.at[j], peer)
        copy.start()
        sends.append(copy)

    def pass_on(t):
        for j, peer in ((1, right), (2, left)):
            copy = remote(
                buf.at[0, t, KV], buf.at[j, t, KV], ysend.at[j - 1, t], yrecv.at[j - 1, t], peer
            )
            copy.start()
            sends.append(copy)

    buf[0, 0] = stage[z]
    pass_on(0)

    own_rows = pl.ds(pl.multiple_of(side * HALF, HALF), HALF)
    shares = []
    for j, t in ((1, 1), (2, 3), (3, 2)):
        copy = remote(
            w_out_hbm.at[own_rows], w_out.at[j, own_rows], wsend.at[j], wrecv.at[j], over(t)
        )
        copy.start()
        shares.append(copy)

    kv9[0] = stage[8]
    q9[0] = stage[8, 0:128, :]
    best_s[...] = jnp.full_like(best_s, NEG_FILL)
    total_s[...] = jnp.zeros_like(total_s)
    accum_s[...] = jnp.zeros_like(accum_s)

    def relay(t, onto, peer):
        ring[t].wait_recv()
        ring[onto] = remote(
            kv9.at[t, KV], kv9.at[onto, KV], rsend.at[onto], rrecv.at[onto], peer
        )
        ring[onto].start()

    owners = owner_ref[...].astype(f32)
    owner_column = jnp.sum(jnp.where(row == lane, owners, 0.0), axis=1, keepdims=True)
    half_start = jnp.where(lane >= HALF, float(HALF), 0.0)
    earlier = (owner_column == owners) & (row < lane) & (row >= half_start)
    ranks = jnp.sum(jnp.where(earlier, 1.0, 0.0), axis=0, keepdims=True)
    owner_y = functools.reduce(
        jnp.add, [jnp.where(owners >= edge, 1.0, 0.0) for edge in (8, 16, 24)]
    )
    target = (owners - 8 * owner_y) * 48 + owner_y * CAP + ranks
    low = side.astype(f32) * HALF
    slot = lane[0:1]
    chosen = (slot < count) & (slot >= low) & (slot < low + HALF)
    target = jnp.where(chosen, target, -1.0)
    by_slot = jnp.where(row == target, 1.0, 0.0).astype(bf16)
    half_perm = jnp.concatenate(
        [perm[pl.ds(pl.multiple_of(c * 128 + side * 64, 64), 64), :] for c in range(CLIPS)], axis=0
    )
    placing[...] = lax.dot_general(
        by_slot, half_perm, (((1,), (1,)), ((), ())), preferred_element_type=f32
    ).astype(bf16)
    from_z = jnp.floor((slot + 0.5) * (1.0 / 48.0))
    within = slot - 48 * from_z
    to_y = jnp.floor((within + 0.5) * (1.0 / CAP))
    repack[...] = jnp.where(
        row == to_y * 96 + from_z * CAP + within - CAP * to_y, 1.0, 0.0
    ).astype(bf16)

    loads[3].wait()
    for k in range(3):
        cols = slice(512 * k, 512 * k + 512)
        mixed[:, cols] = jnp.dot(perm[...], residual[:, cols], preferred_element_type=f32)

    def out_block(problem):
        row = pl.multiple_of((problem % 3) * 128, 128)
        column = pl.multiple_of((problem // 3) * 128, 128)
        return att.at[0, pl.ds(row, 128), pl.ds(column, 128)]

    def returning(t):
        return remote(
            out_stage.at[t], out_block(z), osend.at[t], orecv.at[t], along((Z - t) % Z)
        )

    def from_row(way, t):
        return remote(
            buf.at[0, t, KV], buf.at[1 + way, t, KV],
            ysend.at[way, t], yrecv.at[way, t], (right, left)[way],
        )

    def far_row(t):
        return remote(
            buf.at[1 + t % 2, t, KV], buf.at[3, t, KV],
            ysend.at[2, t], yrecv.at[2, t], (right, left)[t % 2],
        )

    def attend(j, tile):
        rows = pl.ds(pl.multiple_of(tile * 256, 256), 256)
        query = buf[0, pl.ds(2 * tile, 2), 0:128, :].reshape(256, HEAD_DIM)
        best, total, accum = attend_tile(
            query, buf.at[j], best_s[rows, :], total_s[rows, :], accum_s[rows, :]
        )
        best_s[rows, :] = best
        total_s[rows, :] = total
        accum_s[rows, :] = accum
        return total, accum

    def group(j):
        def one(tile, carry):
            attend(j, tile)
            return carry

        lax.fori_loop(0, 4, one, 0)

    for i, t in enumerate(NEAR_FIRST):
        sends[i].wait_recv()
        pass_on(t)
        if i == 1:
            relay(1, 2, along(1))
            relay(7, 6, along(7))
    relay(2, 3, along(1))
    relay(6, 5, along(7))
    group(0)
    relay(3, 4, along(1))
    for t in range(Z):
        for way in (0, 1):
            from_row(way, t).wait_recv()
        far_row(t).start()
    group(1)
    group(2)

    ring[5].wait_recv()
    ring[4].wait_recv()
    for j in (1, 2, 3):
        sends[6 + j].wait_recv()
    corner = lax.broadcasted_iota(jnp.int32, (128, 128), 0) == lax.broadcasted_iota(
        jnp.int32, (128, 128), 1
    )

    def ninth(tile, carry):
        query = q9[pl.ds(2 * tile, 2)].reshape(256, HEAD_DIM)
        zero = jnp.zeros((256, HEAD_DIM), f32)
        best, total, accum = attend_tile(query, kv9, zero + NEG_FILL, zero, zero)
        total = jnp.sum(total, axis=1, keepdims=True)
        part_out[pl.ds(2 * tile, 2)] = (accum / total).astype(bf16).reshape(2, 128, 128)
        for i in range(2):
            rows = slice(128 * i, 128 * i + 128)
            for at, column in ((0, best[rows, 0:1]), (8, total[rows])):
                line = jnp.sum(jnp.where(corner, column, 0.0), axis=0, keepdims=True)
                stat_out[2 * tile + i, at : at + 8, :] = jnp.broadcast_to(line, (8, 128))
        return carry

    lax.fori_loop(0, 2, ninth, 0)
    parts = []
    for j, onto, peer in ((1, 2, left), (2, 1, right), (3, 3, across)):
        for copy in (
            remote(part_out.at[j], part_in.at[onto], psend.at[j], precv.at[onto], peer),
            remote(stat_out.at[j], stat_in.at[onto], ssend.at[j], srecv.at[onto], peer),
        ):
            copy.start()
            parts.append(copy)

    for t in range(Z):
        far_row(t).wait()

    def finish_tile(tile, carry):
        total, accum = attend(3, tile)
        result = accum / jnp.sum(total, axis=1, keepdims=True)
        out_stage[pl.ds(2 * tile, 2)] = result.astype(bf16).reshape(2, 128, 128)

        @pl.when(tile > 0)
        def _():
            returning(2 * tile).start()

        returning(2 * tile + 1).start()
        return carry

    lax.fori_loop(0, 4, finish_tile, 0)
    own_block = pltpu.make_async_copy(out_stage.at[0], out_block(z), osend.at[0])
    own_block.start()

    swaps = []
    for j, copy in enumerate(shares, 1):
        copy.wait()
        swap = remote(
            w_out.at[j, own_rows], w_out.at[j, own_rows], csend.at[j], crecv.at[j], other_core
        )
        swap.start()
        swaps.append(swap)

    for copy in parts:
        copy.wait()
    lines = [stat_out.at[0], stat_in.at[1], stat_in.at[2], stat_in.at[3]]
    pieces = [part_out.at[0], part_in.at[1], part_in.at[2], part_in.at[3]]
    bests = [line[0:1, :] for line in lines]
    top = functools.reduce(jnp.maximum, bests)
    weights = [
        jnp.exp2((best - top) * EXP2_SCALE) * line[8:9, :] for best, line in zip(bests, lines)
    ]
    total = functools.reduce(jnp.add, weights)
    accum = functools.reduce(
        jnp.add,
        [
            jnp.sum(jnp.where(corner, weight / total, 0.0), axis=1, keepdims=True)
            * piece[...].astype(f32)
            for weight, piece in zip(weights, pieces)
        ],
    )
    att[0, 256:384, 256:384] = accum.astype(bf16)

    own_block.wait()
    for t in range(1, Z):
        remote(
            out_stage.at[t], out_block((z + t) % Z), osend.at[t], orecv.at[t], along(Z - t)
        ).wait_recv()

    gathers = {}

    def hop(src, slot, part, peer):
        rows = (TOP, LOW)[part]
        copy = remote(
            att.at[src, rows], att.at[slot, rows], asend.at[slot, part], arecv.at[slot, part], peer
        )
        copy.start()
        gathers[slot, part] = copy

    hop(0, 1, 0, over(1))
    hop(0, 2, 1, over(3))
    hop(0, 1, 1, over(1))
    hop(0, 2, 0, over(3))

    for copy in loads[4:6]:
        copy.wait()
    for copy in swaps:
        copy.wait()

    def project(slot):
        rows = att[slot]

        def one(k, carry):
            cols = pl.ds(pl.multiple_of(k * 512, 512), 512)
            term = jnp.dot(rows, w_out[slot, :, cols], preferred_element_type=f32)
            for c in range(CLIPS):
                part = slice(128 * c, 128 * c + 128)
                mixed[part, cols] += mod[c, 0:1, cols] * term[part]
            return carry

        lax.fori_loop(0, 3, one, 0)

    gathers[1, 0].wait_recv()
    hop(1, 3, 0, over(1))
    gathers[2, 1].wait_recv()
    hop(2, 3, 1, over(3))
    project(0)
    gathers[1, 1].wait_recv()
    project(1)
    gathers[2, 0].wait_recv()
    project(2)
    gathers[3, 0].wait_recv()
    gathers[3, 1].wait_recv()
    project(3)

    def normalise(k, carry):
        for c in range(CLIPS):
            rows = pl.ds(pl.multiple_of(c * 128 + k * 32, 32), 32)
            value = mixed[rows, :]
            centre = value - jnp.mean(value, axis=1, keepdims=True)
            spread = jnp.mean(centre * centre, axis=1, keepdims=True)
            scaled = centre * lax.rsqrt(spread + 1e-06) * (1.0 + mod[c, 2:3, :]) + mod[c, 1:2, :]
            normed[rows, :] = scaled.astype(bf16)
        return carry

    lax.fori_loop(0, 4, normalise, 0)

    loads[6].wait()

    def expand(k, carry):
        cols = pl.ds(pl.multiple_of(k * 512, 512), 512)
        value = jnp.dot(normed[...], w_up[:, cols], preferred_element_type=f32)
        hidden[:, cols] = jax.nn.gelu(value, approximate=True).astype(bf16)
        return carry

    lax.fori_loop(0, 3, expand, 0)

    loads[7].wait()

    def contract(t):
        cols = pl.ds(pl.multiple_of(((blk + t) % X) * SLOTS, SLOTS), SLOTS)
        return jnp.dot(hidden[...], w_down[:, cols], preferred_element_type=f32)

    passing, finals = {}, {}

    def chunk(k):
        return slice(128 * k, 128 * k + 128)

    def give_far():
        far_terms = contract(2).astype(bf16)
        for k in range(3):
            far[k] = far_terms[:, chunk(k)]
            for way, rows in ((0, TOP), (1, LOW)):
                passing[way, k] = remote(
                    far.at[k, rows], transit.at[way, k],
                    tsend.at[way, k], trecv.at[way, k], over((1, 3)[way]),
                )
                passing[way, k].start()

    def give_near(way):
        terms = contract((1, 3)[way])
        low = (HALF, 0)[way]
        for k in range(3):
            near[way, k] = terms[:, chunk(k)]
            ready[1 + way, k] = terms[low : low + HALF, chunk(k)].astype(bf16)
            deliver(1 + way, k)

    def deliver(which, k):
        finals[which, k] = remote(
            ready.at[which, k], final.at[which, k],
            fsend.at[which, k], frecv.at[which, k], over((1, 1, 3, 3)[which]),
        )
        finals[which, k].start()

    def merge(k):
        for way, which, rows in ((0, 0, TOP), (1, 3, LOW)):
            passing[way, k].wait_recv()
            ready[which, k] = (near[way, k, rows, :] + transit[way, k].astype(f32)).astype(bf16)
            deliver(which, k)

    exchanges, trips, last = {}, [], []

    def finish(k):
        for which in range(4):
            finals[which, k].wait_recv()
        cols = pl.ds(pl.multiple_of(blk * SLOTS + 128 * k, 128), 128)
        for c in range(CLIPS):
            for half in range(2):
                start = c * 128 + half * 64
                which, rows = start // HALF, slice(start % HALF, start % HALF + 64)
                summed = own[start : start + 64, chunk(k)] + final[which, k, rows].astype(f32)
                summed = summed + final[2 + which, k, rows].astype(f32)
                value = mixed[start : start + 64, cols] + mod[c, 3:4, cols] * summed
                mine[half, k, c * 64 : c * 64 + 64] = value.astype(bf16)
        exchanges[k] = remote(
            mine.at[1 - side, k], theirs.at[k], esend.at[k], erecv.at[k], other_core
        )
        exchanges[k].start()

    here = pl.ds(pl.multiple_of(z * 48, 16), 48)

    def send_rows(k):
        exchanges[k].wait_recv()
        ours, others = mine[side, k].astype(f32), theirs[k].astype(f32)
        conditional = jnp.where(side == 0, ours, others)
        plain = jnp.where(side == 0, others, ours)
        guided = jnp.concatenate(
            [
                plain[64 * c : 64 * c + 64]
                + guide_ref[c] * (conditional[64 * c : 64 * c + 64] - plain[64 * c : 64 * c + 64])
                for c in range(CLIPS)
            ],
            axis=0,
        ).astype(bf16)
        going[k] = jnp.dot(placing[...], guided, preferred_element_type=f32).astype(bf16)
        for t in NEAR_FIRST:
            there = pl.ds(pl.multiple_of(((z + t) % Z) * 48, 16), 48)
            copy = remote(
                going.at[k, there], landed.at[k, here], gsend.at[k, t], grecv.at[k, t], along(t)
            )
            copy.start()
            trips.append(copy)
        landed[k, here, :] = going[k, here, :]

    row_here = pl.ds(pl.multiple_of(y * 96, 96), 96)

    def turn_rows(k):
        cols = pl.ds(128 * k, 128)
        for copy in trips[7 * k : 7 * k + 7]:
            copy.wait_recv()
        turned[k] = jnp.dot(repack[...], landed[k], preferred_element_type=f32).astype(bf16)
        for t in (1, 3, 2):
            there = pl.ds(pl.multiple_of(((y + t) % Y) * 96, 96), 96)
            copy = remote(
                turned.at[k, there], out_ref.at[0, row_here, cols],
                hsend.at[k, t], hrecv.at[k, t], up(t),
            )
            copy.start()
            last.append(copy)
        out_ref[0, row_here, 128 * k : 128 * k + 128] = turned[k, row_here, :]

    give_far()
    give_near(0)
    give_near(1)
    merge(0)
    merge(1)
    merge(2)
    own = contract(0)
    finish(0)
    finish(1)
    send_rows(0)
    finish(2)
    send_rows(1)
    turn_rows(0)
    send_rows(2)
    turn_rows(1)
    turn_rows(2)
    for copy in last:
        copy.wait()

    for t in range(1, Z):
        returning(t).wait_send()
    for copy in [
        *sends, *ring.values(), *gathers.values(), *passing.values(), *finals.values(),
        *exchanges.values(), *trips,
    ]:
        copy.wait_send()


def block(clips, owners, guide_scale, *arrays):
    dma = pltpu.SemaphoreType.DMA
    vmem = pltpu.VMEM
    f32, bf16 = jnp.float32, jnp.bfloat16
    return pl.pallas_call(
        block_kernel,
        out_shape=jax.ShapeDtypeStruct((1, SLOTS, SLOTS), bf16),
        in_specs=[
            pl.BlockSpec(memory_space=vmem),
            pl.BlockSpec(memory_space=vmem),
            pl.BlockSpec(memory_space=pltpu.SMEM),
            *[pl.BlockSpec(memory_space=pl.ANY)] * 8,
        ],
        out_specs=pl.BlockSpec(memory_space=vmem),
        scratch_shapes=[
            vmem((3, SLOTS, SLOTS), bf16),
            vmem((SLOTS, SLOTS), bf16),
            vmem((9, MSG, 128), bf16),
            vmem((4, Z, MSG, 128), bf16),
            vmem((Z, MSG, 128), bf16),
            vmem((4, 128, 128), bf16),
            vmem((4, 128, 128), bf16),
            vmem((4, 128, 128), bf16),
            vmem((4, 16, 128), f32),
            vmem((4, 16, 128), f32),
            vmem((1024, 128), f32),
            vmem((1024, 128), f32),
            vmem((1024, 128), f32),
            vmem((Z, 128, 128), bf16),
            vmem((4, SLOTS, SLOTS), bf16),
            vmem((4, SLOTS, D), bf16),
            vmem((D, D), bf16),
            vmem((D, D), bf16),
            vmem((SLOTS, D), bf16),
            vmem((CLIPS, 4, D), f32),
            vmem((SLOTS, D), f32),
            vmem((SLOTS, D), bf16),
            vmem((SLOTS, D), bf16),
            vmem((3, SLOTS, 128), bf16),
            vmem((2, 3, SLOTS, 128), f32),
            vmem((4, 3, HALF, 128), bf16),
            vmem((2, 3, HALF, 128), bf16),
            vmem((4, 3, HALF, 128), bf16),
            vmem((2, 3, HALF, 128), bf16),
            vmem((3, HALF, 128), bf16),
            vmem((SLOTS, HALF), bf16),
            vmem((SLOTS, SLOTS), bf16),
            vmem((3, SLOTS, 128), bf16),
            vmem((3, SLOTS, 128), bf16),
            vmem((3, SLOTS, 128), bf16),
            dma((8,)),
            *[dma((Z,))] * 4,
            *[dma((3, Z))] * 2,
            *[dma((4,))] * 6,
            *[dma((Z,))] * 2,
            *[dma((4,))] * 4,
            *[dma((4, 2))] * 2,
            *[dma((2, 3))] * 2,
            *[dma((4, 3))] * 2,
            *[dma((3,))] * 2,
            *[dma((3, Z))] * 2,
            *[dma((3, Y))] * 2,
        ],
        compiler_params=pltpu.CompilerParams(
            collective_id=0, has_side_effects=True, vmem_limit_bytes=56 * 2**20
        ),
        name="guided_block",
    )(clips, owners, guide_scale, *arrays)


def shards(
    queries, keys, values, residual, w_out, w_up, w_down, modulation, guide_scale, slot_clip, owner
):
    return block(
        slot_clip.reshape(1, SLOTS),
        owner.reshape(1, SLOTS),
        guide_scale,
        queries,
        keys,
        values,
        residual,
        modulation,
        w_out,
        w_up,
        w_down,
    )


def solution(mesh):
    placed = (
        P("cfg", "seq", "blk"),
        P("cfg", "seq", "blk"),
        P("cfg", "seq", "blk"),
        P("cfg", "seq", None),
        P("blk", None),
        P(None, "blk"),
        P("blk", None),
        P(),
        P(),
        P("seq"),
        P("seq", None),
    )
    return jax.shard_map(
        shards, mesh=mesh, in_specs=placed, out_specs=P("cfg", "seq", "blk"), check_vma=False
    )
```

```python
import functools
import math

import jax
import jax.numpy as jnp
from jax import lax
from jax.experimental import pallas as pl
from jax.experimental.pallas import tpu as pltpu
from jax.sharding import PartitionSpec as P

D = 1536
HEAD_DIM = 128
CLIPS = 3
HEADS_HERE = 3
GROUP = 128
Y, Z = 4, 8
MSG = 400
KV = pl.ds(128, 272)
NEG_FILL = -1e30
EXP2_SCALE = math.log2(math.e) / math.sqrt(HEAD_DIM)
MESH = pl.DeviceIdType.MESH
NEAR_FIRST = (1, 7, 2, 6, 3, 5, 4)
X = 4
SLOTS = 384
HALF = 192
CAP = 12
TOP, LOW = pl.ds(0, HALF), pl.ds(HALF, HALF)


def remote(src, dst, send, recv, peer):
    return pltpu.make_async_remote_copy(
        src_ref=src,
        dst_ref=dst,
        send_sem=send,
        recv_sem=recv,
        device_id=peer,
        device_id_type=MESH,
    )


def attend_tile(query, kv, best, total, accum):
    count = kv.shape[0]
    keys = kv[:, 128:256, :].reshape(count * GROUP, HEAD_DIM)
    scores = lax.dot_general(
        query, keys, (((1,), (1,)), ((), ())), preferred_element_type=jnp.float32
    )
    pieces = []
    for i in range(count):
        bias = kv[i, 384:400, :].astype(jnp.float32)[0:1]
        pieces.append(scores[:, i * GROUP : (i + 1) * GROUP] + bias)
    peak = functools.reduce(jnp.maximum, pieces)
    new_best = jnp.maximum(best, jnp.max(peak, axis=1, keepdims=True))
    probs = [jnp.exp2((piece - new_best) * EXP2_SCALE) for piece in pieces]
    fade = jnp.exp2((best - new_best) * EXP2_SCALE)
    total = total * fade + functools.reduce(jnp.add, probs)
    weights = jnp.concatenate([prob.astype(jnp.bfloat16) for prob in probs], axis=1)
    values = kv[:, 256:384, :].reshape(count * GROUP, HEAD_DIM)
    accum = accum * fade + jnp.dot(weights, values, preferred_element_type=jnp.float32)
    return new_best, total, accum


def block_kernel(
    clip_ref,
    owner_ref,
    guide_ref,
    q_hbm,
    k_hbm,
    v_hbm,
    res_hbm,
    mod_hbm,
    w_out_hbm,
    w_up_hbm,
    w_down_hbm,
    out_ref,
    qkv,
    perm,
    stage,
    buf,
    kv9,
    q9,
    part_out,
    part_in,
    stat_out,
    stat_in,
    best_s,
    total_s,
    accum_s,
    out_stage,
    att,
    w_out,
    w_up,
    w_down,
    residual,
    mod,
    mixed,
    normed,
    hidden,
    far,
    near,
    ready,
    transit,
    final,
    mine,
    base,
    placing,
    repack,
    going,
    landed,
    turned,
    lsem,
    zsend,
    zrecv,
    rsend,
    rrecv,
    ysend,
    yrecv,
    qsend,
    qrecv,
    psend,
    precv,
    ssend,
    srecv,
    osend,
    orecv,
    wsend,
    wrecv,
    csend,
    crecv,
    asend,
    arecv,
    tsend,
    trecv,
    fsend,
    frecv,
    esend,
    erecv,
    gsend,
    grecv,
    hsend,
    hrecv,
):
    f32, bf16 = jnp.float32, jnp.bfloat16
    me = lax.axis_index("seq")
    side = lax.axis_index("cfg")
    blk = lax.axis_index("blk")
    y, z = me // Z, me % Z

    def up(t):
        return {"seq": ((y + t) % Y) * Z + z}

    def along(t):
        return {"seq": y * Z + (z + t) % Z}

    def over(t):
        return {"blk": (blk + t) % X}

    right, left, across = up(1), up(3), up(2)
    other_core = {"cfg": 1 - side}

    barrier = pltpu.get_barrier_semaphore()
    peers = [along(t) for t in range(1, Z)] + [up(t) for t in range(1, Y)]
    peers += [over(t) for t in range(1, X)] + [other_core]
    peers += [{**over(t), **other_core} for t in (1, 3)]
    for peer in peers:
        pl.semaphore_signal(barrier, inc=1, device_id=peer, device_id_type=MESH)

    loads = [
        pltpu.make_async_copy(src, dst, lsem.at[i])
        for i, (src, dst) in enumerate(
            (
                (q_hbm.at[0], qkv.at[0]),
                (k_hbm.at[0], qkv.at[1]),
                (v_hbm.at[0], qkv.at[2]),
                (res_hbm.at[0], residual),
                (mod_hbm, mod),
                (w_out_hbm, w_out.at[0]),
                (w_up_hbm, w_up),
                (w_down_hbm, w_down),
            )
        )
    ]
    for copy in loads:
        copy.start()

    clips = clip_ref[...].astype(f32)
    first = clips[0:1, 0:1]
    count = jnp.sum(jnp.where(clips < CLIPS, 1.0, 0.0), axis=1, keepdims=True)
    row = lax.broadcasted_iota(jnp.int32, (SLOTS, SLOTS), 0).astype(f32)
    lane = lax.broadcasted_iota(jnp.int32, (SLOTS, SLOTS), 1).astype(f32)
    row_clip = jnp.where(row >= 128, 1.0, 0.0) + jnp.where(row >= 256, 1.0, 0.0)
    step = row_clip - first
    step = jnp.where(step < 0, step + 3, step)
    perm[...] = jnp.where(3 * (row - 128 * row_clip) + step == lane, 1.0, 0.0).astype(bf16)
    rank = lax.broadcasted_iota(jnp.int32, (16, 128), 1).astype(f32)
    for c in range(CLIPS):
        step = c - first
        step = jnp.where(step < 0, step + 3, step)
        bias = jnp.where(3 * rank + step < count, 0.0, NEG_FILL).astype(bf16)
        for h in range(HEADS_HERE):
            stage[3 * h + c, 384:400, :] = bias

    for which in range(3):
        loads[which].wait()
        rows = jnp.dot(perm[...], qkv[which], preferred_element_type=f32).astype(bf16)
        for h in range(HEADS_HERE):
            for c in range(CLIPS):
                stage[3 * h + c, which * 128 : which * 128 + 128, :] = rows[
                    c * 128 : c * 128 + 128, h * 128 : h * 128 + 128
                ]

    pl.semaphore_wait(barrier, len(peers))

    ring = {
        1: remote(stage.at[8, KV], kv9.at[1, KV], rsend.at[1], rrecv.at[1], along(1)),
        7: remote(stage.at[8, KV], kv9.at[7, KV], rsend.at[7], rrecv.at[7], along(7)),
    }
    for copy in ring.values():
        copy.start()
    sends = []
    for t in NEAR_FIRST:
        copy = remote(
            stage.at[(z + t) % Z], buf.at[0, t], zsend.at[t], zrecv.at[t], along(t)
        )
        copy.start()
        sends.append(copy)
    for j, peer in ((1, right), (2, left), (3, across)):
        copy = remote(stage.at[8, pl.ds(0, 128)], q9.at[j], qsend.at[j], qrecv.at[j], peer)
        copy.start()
        sends.append(copy)

    def pass_on(t):
        for j, peer in ((1, right), (2, left)):
            copy = remote(
                buf.at[0, t, KV], buf.at[j, t, KV], ysend.at[j - 1, t], yrecv.at[j - 1, t], peer
            )
            copy.start()
            sends.append(copy)

    buf[0, 0] = stage[z]
    pass_on(0)

    own_rows = pl.ds(pl.multiple_of(side * HALF, HALF), HALF)
    shares = []
    for j, t in ((1, 1), (2, 3), (3, 2)):
        copy = remote(
            w_out_hbm.at[own_rows], w_out.at[j, own_rows], wsend.at[j], wrecv.at[j], over(t)
        )
        copy.start()
        shares.append(copy)

    kv9[0] = stage[8]
    q9[0] = stage[8, 0:128, :]
    best_s[...] = jnp.full_like(best_s, NEG_FILL)
    total_s[...] = jnp.zeros_like(total_s)
    accum_s[...] = jnp.zeros_like(accum_s)

    def relay(t, onto, peer):
        ring[t].wait_recv()
        ring[onto] = remote(
            kv9.at[t, KV], kv9.at[onto, KV], rsend.at[onto], rrecv.at[onto], peer
        )
        ring[onto].start()

    owners = owner_ref[...].astype(f32)
    owner_column = jnp.sum(jnp.where(row == lane, owners, 0.0), axis=1, keepdims=True)
    half_start = jnp.where(lane >= HALF, float(HALF), 0.0)
    earlier = (owner_column == owners) & (row < lane) & (row >= half_start)
    ranks = jnp.sum(jnp.where(earlier, 1.0, 0.0), axis=0, keepdims=True)
    owner_y = functools.reduce(
        jnp.add, [jnp.where(owners >= edge, 1.0, 0.0) for edge in (8, 16, 24)]
    )
    target = (owners - 8 * owner_y) * 48 + owner_y * CAP + ranks
    low = side.astype(f32) * HALF
    slot = lane[0:1]
    chosen = (slot < count) & (slot >= low) & (slot < low + HALF)
    target = jnp.where(chosen, target, -1.0)
    by_slot = jnp.where(row == target, 1.0, 0.0).astype(bf16)
    half_perm = jnp.concatenate(
        [perm[pl.ds(pl.multiple_of(c * 128 + side * 64, 64), 64), :] for c in range(CLIPS)], axis=0
    )
    placing[...] = lax.dot_general(
        by_slot, half_perm, (((1,), (1,)), ((), ())), preferred_element_type=f32
    ).astype(bf16)
    from_z = jnp.floor((slot + 0.5) * (1.0 / 48.0))
    within = slot - 48 * from_z
    to_y = jnp.floor((within + 0.5) * (1.0 / CAP))
    repack[...] = jnp.where(
        row == to_y * 96 + from_z * CAP + within - CAP * to_y, 1.0, 0.0
    ).astype(bf16)

    loads[3].wait()
    for k in range(3):
        cols = slice(512 * k, 512 * k + 512)
        mixed[:, cols] = jnp.dot(perm[...], residual[:, cols], preferred_element_type=f32)

    def out_block(problem):
        row = pl.multiple_of((problem % 3) * 128, 128)
        column = pl.multiple_of((problem // 3) * 128, 128)
        return att.at[0, pl.ds(row, 128), pl.ds(column, 128)]

    def returning(t):
        return remote(
            out_stage.at[t], out_block(z), osend.at[t], orecv.at[t], along((Z - t) % Z)
        )

    def from_row(way, t):
        return remote(
            buf.at[0, t, KV], buf.at[1 + way, t, KV],
            ysend.at[way, t], yrecv.at[way, t], (right, left)[way],
        )

    def far_row(t):
        return remote(
            buf.at[1 + t % 2, t, KV], buf.at[3, t, KV],
            ysend.at[2, t], yrecv.at[2, t], (right, left)[t % 2],
        )

    def attend(j, tile):
        rows = pl.ds(pl.multiple_of(tile * 256, 256), 256)
        query = buf[0, pl.ds(2 * tile, 2), 0:128, :].reshape(256, HEAD_DIM)
        best, total, accum = attend_tile(
            query, buf.at[j], best_s[rows, :], total_s[rows, :], accum_s[rows, :]
        )
        best_s[rows, :] = best
        total_s[rows, :] = total
        accum_s[rows, :] = accum
        return total, accum

    def group(j):
        def one(tile, carry):
            attend(j, tile)
            return carry

        lax.fori_loop(0, 4, one, 0)

    for i, t in enumerate(NEAR_FIRST):
        sends[i].wait_recv()
        pass_on(t)
        if i == 1:
            relay(1, 2, along(1))
            relay(7, 6, along(7))
    relay(2, 3, along(1))
    relay(6, 5, along(7))
    group(0)
    relay(3, 4, along(1))
    for t in range(Z):
        for way in (0, 1):
            from_row(way, t).wait_recv()
        far_row(t).start()
    group(1)
    group(2)

    ring[5].wait_recv()
    ring[4].wait_recv()
    for j in (1, 2, 3):
        sends[6 + j].wait_recv()
    corner = lax.broadcasted_iota(jnp.int32, (128, 128), 0) == lax.broadcasted_iota(
        jnp.int32, (128, 128), 1
    )

    def ninth(tile, carry):
        query = q9[pl.ds(2 * tile, 2)].reshape(256, HEAD_DIM)
        zero = jnp.zeros((256, HEAD_DIM), f32)
        best, total, accum = attend_tile(query, kv9, zero + NEG_FILL, zero, zero)
        total = jnp.sum(total, axis=1, keepdims=True)
        part_out[pl.ds(2 * tile, 2)] = (accum / total).astype(bf16).reshape(2, 128, 128)
        for i in range(2):
            rows = slice(128 * i, 128 * i + 128)
            for at, column in ((0, best[rows, 0:1]), (8, total[rows])):
                line = jnp.sum(jnp.where(corner, column, 0.0), axis=0, keepdims=True)
                stat_out[2 * tile + i, at : at + 8, :] = jnp.broadcast_to(line, (8, 128))
        return carry

    lax.fori_loop(0, 2, ninth, 0)
    parts = []
    for j, onto, peer in ((1, 2, left), (2, 1, right), (3, 3, across)):
        for copy in (
            remote(part_out.at[j], part_in.at[onto], psend.at[j], precv.at[onto], peer),
            remote(stat_out.at[j], stat_in.at[onto], ssend.at[j], srecv.at[onto], peer),
        ):
            copy.start()
            parts.append(copy)

    for t in range(Z):
        far_row(t).wait()

    def finish_tile(tile, carry):
        total, accum = attend(3, tile)
        result = accum / jnp.sum(total, axis=1, keepdims=True)
        out_stage[pl.ds(2 * tile, 2)] = result.astype(bf16).reshape(2, 128, 128)

        @pl.when(tile > 0)
        def _():
            returning(2 * tile).start()

        returning(2 * tile + 1).start()
        return carry

    lax.fori_loop(0, 4, finish_tile, 0)
    own_block = pltpu.make_async_copy(out_stage.at[0], out_block(z), osend.at[0])
    own_block.start()

    swaps = []
    for j, copy in enumerate(shares, 1):
        copy.wait()
        swap = remote(
            w_out.at[j, own_rows], w_out.at[j, own_rows], csend.at[j], crecv.at[j], other_core
        )
        swap.start()
        swaps.append(swap)

    for copy in parts:
        copy.wait()
    lines = [stat_out.at[0], stat_in.at[1], stat_in.at[2], stat_in.at[3]]
    pieces = [part_out.at[0], part_in.at[1], part_in.at[2], part_in.at[3]]
    bests = [line[0:1, :] for line in lines]
    top = functools.reduce(jnp.maximum, bests)
    weights = [
        jnp.exp2((best - top) * EXP2_SCALE) * line[8:9, :] for best, line in zip(bests, lines)
    ]
    total = functools.reduce(jnp.add, weights)
    accum = functools.reduce(
        jnp.add,
        [
            jnp.sum(jnp.where(corner, weight / total, 0.0), axis=1, keepdims=True)
            * piece[...].astype(f32)
            for weight, piece in zip(weights, pieces)
        ],
    )
    att[0, 256:384, 256:384] = accum.astype(bf16)

    own_block.wait()
    for t in range(1, Z):
        remote(
            out_stage.at[t], out_block((z + t) % Z), osend.at[t], orecv.at[t], along(Z - t)
        ).wait_recv()

    gathers = {}

    def hop(src, slot, part, peer):
        rows = (TOP, LOW)[part]
        copy = remote(
            att.at[src, rows], att.at[slot, rows], asend.at[slot, part], arecv.at[slot, part], peer
        )
        copy.start()
        gathers[slot, part] = copy

    hop(0, 1, 0, over(1))
    hop(0, 2, 1, over(3))
    hop(0, 1, 1, over(1))
    hop(0, 2, 0, over(3))

    for copy in loads[4:6]:
        copy.wait()
    for copy in swaps:
        copy.wait()

    def project(slot):
        rows = att[slot]

        def one(k, carry):
            cols = pl.ds(pl.multiple_of(k * 512, 512), 512)
            term = jnp.dot(rows, w_out[slot, :, cols], preferred_element_type=f32)
            for c in range(CLIPS):
                part = slice(128 * c, 128 * c + 128)
                mixed[part, cols] += mod[c, 0:1, cols] * term[part]
            return carry

        lax.fori_loop(0, 3, one, 0)

    gathers[1, 0].wait_recv()
    hop(1, 3, 0, over(1))
    gathers[2, 1].wait_recv()
    hop(2, 3, 1, over(3))
    project(0)
    gathers[1, 1].wait_recv()
    project(1)
    gathers[2, 0].wait_recv()
    project(2)
    gathers[3, 0].wait_recv()
    gathers[3, 1].wait_recv()
    project(3)

    def normalise(k, carry):
        for c in range(CLIPS):
            rows = pl.ds(pl.multiple_of(c * 128 + k * 32, 32), 32)
            value = mixed[rows, :]
            centre = value - jnp.mean(value, axis=1, keepdims=True)
            spread = jnp.mean(centre * centre, axis=1, keepdims=True)
            scaled = centre * lax.rsqrt(spread + 1e-06) * (1.0 + mod[c, 2:3, :]) + mod[c, 1:2, :]
            to = pl.multiple_of((k // 2) * HALF + c * 64 + (k % 2) * 32, 32)
            normed[pl.ds(to, 32), :] = scaled.astype(bf16)
        return carry

    lax.fori_loop(0, 4, normalise, 0)

    loads[6].wait()

    def expand(k, carry):
        cols = pl.ds(pl.multiple_of(k * 512, 512), 512)
        value = jnp.dot(normed[...], w_up[:, cols], preferred_element_type=f32)
        hidden[:, cols] = jax.nn.gelu(value, approximate=True).astype(bf16)
        return carry

    lax.fori_loop(0, 3, expand, 0)

    loads[7].wait()

    def contract(t):
        cols = pl.ds(pl.multiple_of(((blk + t) % X) * SLOTS, SLOTS), SLOTS)
        return jnp.dot(hidden[...], w_down[:, cols], preferred_element_type=f32)

    passing, finals = {}, {}

    def chunk(k):
        return slice(128 * k, 128 * k + 128)

    def give_far(k):
        for way, rows in ((0, TOP), (1, LOW)):
            passing[way, k] = remote(
                far.at[k, rows], transit.at[way, k],
                tsend.at[way, k], trecv.at[way, k], over((1, 3)[way]),
            )
            passing[way, k].start()

    def near_terms(way):
        terms = contract((1, 3)[way])
        low = (HALF, 0)[way]
        for k in range(3):
            near[way, k] = terms[:, chunk(k)]
            ready[1 + way, k] = terms[low : low + HALF, chunk(k)].astype(bf16)

    def deliver(which, k):
        finals[which, k] = remote(
            ready.at[which, k], final.at[side, which // 2, k],
            fsend.at[which, k], frecv.at[side, which // 2, k],
            {**over((1, 1, 3, 3)[which]), "cfg": which % 2},
        )
        finals[which, k].start()

    def merge(k):
        for way, which, rows in ((0, 0, TOP), (1, 3, LOW)):
            passing[way, k].wait_recv()
            ready[which, k] = (near[way, k, rows, :] + transit[way, k].astype(f32)).astype(bf16)
            deliver(which, k)

    trips, last = [], []
    here = pl.ds(pl.multiple_of(z * 48, 16), 48)

    def send_rows(k):
        cols = pl.ds(pl.multiple_of(blk * SLOTS + 128 * k, 128), 128)
        for source in range(2):
            for way in range(2):
                remote(
                    ready.at[way, k], final.at[source, way, k],
                    fsend.at[way, k], frecv.at[source, way, k], over(1),
                ).wait_recv()
        guided = []
        for c in range(CLIPS):
            rows = slice(64 * c, 64 * c + 64)
            cond, uncond = (
                (
                    base[source, rows, chunk(k)]
                    + mod[c, 3:4, cols]
                    * (final[source, 0, k, rows].astype(f32) + final[source, 1, k, rows].astype(f32))
                )
                .astype(bf16)
                .astype(f32)
                for source in range(2)
            )
            guided.append((uncond + guide_ref[c] * (cond - uncond)).astype(bf16))
        guided = jnp.concatenate(guided, axis=0)
        going[k] = jnp.dot(placing[...], guided, preferred_element_type=f32).astype(bf16)
        for t in NEAR_FIRST:
            there = pl.ds(pl.multiple_of(((z + t) % Z) * 48, 16), 48)
            copy = remote(
                going.at[k, there], landed.at[k, here], gsend.at[k, t], grecv.at[k, t], along(t)
            )
            copy.start()
            trips.append(copy)
        landed[k, here, :] = going[k, here, :]

    row_here = pl.ds(pl.multiple_of(y * 96, 96), 96)

    def turn_rows(k):
        cols = pl.ds(128 * k, 128)
        for copy in trips[7 * k : 7 * k + 7]:
            copy.wait_recv()
        turned[k] = jnp.dot(repack[...], landed[k], preferred_element_type=f32).astype(bf16)
        for t in (1, 3, 2):
            there = pl.ds(pl.multiple_of(((y + t) % Y) * 96, 96), 96)
            copy = remote(
                turned.at[k, there], out_ref.at[0, row_here, cols],
                hsend.at[k, t], hrecv.at[k, t], up(t),
            )
            copy.start()
            last.append(copy)
        out_ref[0, row_here, 128 * k : 128 * k + 128] = turned[k, row_here, :]

    far_terms = contract(2).astype(bf16)
    for k in range(3):
        far[k] = far_terms[:, chunk(k)]
    give_far(0)
    give_far(1)
    for way in range(2):
        near_terms(way)
        deliver(1 + way, 0)
    own = contract(0)
    own_cols = pl.ds(pl.multiple_of(blk * SLOTS, SLOTS), SLOTS)
    for half in range(2):
        for c in range(CLIPS):
            at, start = c * 64, c * 128 + half * 64
            mine[half, at : at + 64, :] = (
                mixed[start : start + 64, own_cols]
                + mod[c, 3:4, own_cols] * own[half * HALF + at : half * HALF + at + 64]
            )
    exchange = remote(mine.at[1 - side], base.at[side], esend.at[0], erecv.at[0], other_core)
    exchange.start()
    base[side] = mine[side]

    merge(0)
    give_far(2)
    deliver(1, 1)
    deliver(2, 1)
    merge(1)
    deliver(1, 2)
    deliver(2, 2)
    remote(mine.at[side], base.at[1 - side], esend.at[0], erecv.at[0], other_core).wait_recv()
    send_rows(0)
    merge(2)
    send_rows(1)
    send_rows(2)
    turn_rows(0)
    turn_rows(1)
    turn_rows(2)
    for copy in last:
        copy.wait()

    for t in range(1, Z):
        returning(t).wait_send()
    for copy in [
        *sends, *ring.values(), *gathers.values(), *passing.values(), *finals.values(),
        exchange, *trips,
    ]:
        copy.wait_send()


def block(clips, owners, guide_scale, *arrays):
    dma = pltpu.SemaphoreType.DMA
    vmem = pltpu.VMEM
    f32, bf16 = jnp.float32, jnp.bfloat16
    return pl.pallas_call(
        block_kernel,
        out_shape=jax.ShapeDtypeStruct((1, SLOTS, SLOTS), bf16),
        in_specs=[
            pl.BlockSpec(memory_space=vmem),
            pl.BlockSpec(memory_space=vmem),
            pl.BlockSpec(memory_space=pltpu.SMEM),
            *[pl.BlockSpec(memory_space=pl.ANY)] * 8,
        ],
        out_specs=pl.BlockSpec(memory_space=vmem),
        scratch_shapes=[
            vmem((3, SLOTS, SLOTS), bf16),
            vmem((SLOTS, SLOTS), bf16),
            vmem((9, MSG, 128), bf16),
            vmem((4, Z, MSG, 128), bf16),
            vmem((Z, MSG, 128), bf16),
            vmem((4, 128, 128), bf16),
            vmem((4, 128, 128), bf16),
            vmem((4, 128, 128), bf16),
            vmem((4, 16, 128), f32),
            vmem((4, 16, 128), f32),
            vmem((1024, 128), f32),
            vmem((1024, 128), f32),
            vmem((1024, 128), f32),
            vmem((Z, 128, 128), bf16),
            vmem((4, SLOTS, SLOTS), bf16),
            vmem((4, SLOTS, D), bf16),
            vmem((D, D), bf16),
            vmem((D, D), bf16),
            vmem((SLOTS, D), bf16),
            vmem((CLIPS, 4, D), f32),
            vmem((SLOTS, D), f32),
            vmem((SLOTS, D), bf16),
            vmem((SLOTS, D), bf16),
            vmem((3, SLOTS, 128), bf16),
            vmem((2, 3, SLOTS, 128), f32),
            vmem((4, 3, HALF, 128), bf16),
            vmem((2, 3, HALF, 128), bf16),
            vmem((2, 2, 3, HALF, 128), bf16),
            vmem((2, HALF, SLOTS), f32),
            vmem((2, HALF, SLOTS), f32),
            vmem((SLOTS, HALF), bf16),
            vmem((SLOTS, SLOTS), bf16),
            vmem((3, SLOTS, 128), bf16),
            vmem((3, SLOTS, 128), bf16),
            vmem((3, SLOTS, 128), bf16),
            dma((8,)),
            *[dma((Z,))] * 4,
            *[dma((3, Z))] * 2,
            *[dma((4,))] * 6,
            *[dma((Z,))] * 2,
            *[dma((4,))] * 4,
            *[dma((4, 2))] * 2,
            *[dma((2, 3))] * 2,
            dma((4, 3)),
            dma((2, 2, 3)),
            *[dma((1,))] * 2,
            *[dma((3, Z))] * 2,
            *[dma((3, Y))] * 2,
        ],
        compiler_params=pltpu.CompilerParams(
            collective_id=0, has_side_effects=True, vmem_limit_bytes=56 * 2**20
        ),
        name="guided_block",
    )(clips, owners, guide_scale, *arrays)


def shards(
    queries, keys, values, residual, w_out, w_up, w_down, modulation, guide_scale, slot_clip, owner
):
    return block(
        slot_clip.reshape(1, SLOTS),
        owner.reshape(1, SLOTS),
        guide_scale,
        queries,
        keys,
        values,
        residual,
        modulation,
        w_out,
        w_up,
        w_down,
    )


def solution(mesh):
    placed = (
        P("cfg", "seq", "blk"),
        P("cfg", "seq", "blk"),
        P("cfg", "seq", "blk"),
        P("cfg", "seq", None),
        P("blk", None),
        P(None, "blk"),
        P("blk", None),
        P(),
        P(),
        P("seq"),
        P("seq", None),
    )
    return jax.shard_map(
        shards, mesh=mesh, in_specs=placed, out_specs=P("cfg", "seq", "blk"), check_vma=False
    )
```

```python
import functools
import math

import jax
import jax.numpy as jnp
from jax import lax
from jax.experimental import pallas as pl
from jax.experimental.pallas import tpu as pltpu
from jax.sharding import PartitionSpec as P

D = 1536
HEAD_DIM = 128
CLIPS = 3
HEADS_HERE = 3
GROUP = 128
Y, Z = 4, 8
MSG = 400
KV = pl.ds(128, 272)
NEG_FILL = -1e30
EXP2_SCALE = math.log2(math.e) / math.sqrt(HEAD_DIM)
MESH = pl.DeviceIdType.MESH
NEAR_FIRST = (1, 7, 2, 6, 3, 5, 4)
X = 4
SLOTS = 384
HALF = 192
CAP = 12
TOP, LOW = pl.ds(0, HALF), pl.ds(HALF, HALF)


def remote(src, dst, send, recv, peer):
    return pltpu.make_async_remote_copy(
        src_ref=src,
        dst_ref=dst,
        send_sem=send,
        recv_sem=recv,
        device_id=peer,
        device_id_type=MESH,
    )


def attend_tile(query, kv, best, total, accum):
    count = kv.shape[0]
    keys = kv[:, 128:256, :].reshape(count * GROUP, HEAD_DIM)
    scores = lax.dot_general(
        query, keys, (((1,), (1,)), ((), ())), preferred_element_type=jnp.float32
    )
    pieces = []
    for i in range(count):
        bias = kv[i, 384:400, :].astype(jnp.float32)[0:1]
        pieces.append(scores[:, i * GROUP : (i + 1) * GROUP] + bias)
    peak = functools.reduce(jnp.maximum, pieces)
    new_best = jnp.maximum(best, jnp.max(peak, axis=1, keepdims=True))
    probs = [jnp.exp2((piece - new_best) * EXP2_SCALE) for piece in pieces]
    fade = jnp.exp2((best - new_best) * EXP2_SCALE)
    total = total * fade + functools.reduce(jnp.add, probs)
    weights = jnp.concatenate([prob.astype(jnp.bfloat16) for prob in probs], axis=1)
    values = kv[:, 256:384, :].reshape(count * GROUP, HEAD_DIM)
    accum = accum * fade + jnp.dot(weights, values, preferred_element_type=jnp.float32)
    return new_best, total, accum


def block_kernel(
    clip_ref,
    owner_ref,
    guide_ref,
    q_hbm,
    k_hbm,
    v_hbm,
    res_hbm,
    mod_hbm,
    w_out_hbm,
    w_up_hbm,
    w_down_hbm,
    out_ref,
    qkv,
    perm,
    stage,
    buf,
    kv9,
    q9,
    part_out,
    part_in,
    stat_out,
    stat_in,
    best_s,
    total_s,
    accum_s,
    out_stage,
    att,
    w_out,
    w_up,
    w_down,
    residual,
    mod,
    mixed,
    normed,
    hidden,
    far,
    near,
    ready,
    transit,
    final,
    mine,
    base,
    placing,
    repack,
    going,
    landed,
    turned,
    lsem,
    zsend,
    zrecv,
    rsend,
    rrecv,
    ysend,
    yrecv,
    qsend,
    qrecv,
    psend,
    precv,
    ssend,
    srecv,
    osend,
    orecv,
    wsend,
    wrecv,
    csend,
    crecv,
    asend,
    arecv,
    tsend,
    trecv,
    fsend,
    frecv,
    esend,
    erecv,
    gsend,
    grecv,
    hsend,
    hrecv,
):
    f32, bf16 = jnp.float32, jnp.bfloat16
    me = lax.axis_index("seq")
    side = lax.axis_index("cfg")
    blk = lax.axis_index("blk")
    y, z = me // Z, me % Z

    def up(t):
        return {"seq": ((y + t) % Y) * Z + z}

    def along(t):
        return {"seq": y * Z + (z + t) % Z}

    def over(t):
        return {"blk": (blk + t) % X}

    right, left, across = up(1), up(3), up(2)
    other_core = {"cfg": 1 - side}

    barrier = pltpu.get_barrier_semaphore()
    peers = [along(t) for t in range(1, Z)] + [up(t) for t in range(1, Y)]
    peers += [over(t) for t in range(1, X)] + [other_core]
    peers += [{**over(t), **other_core} for t in (1, 3)]
    for peer in peers:
        pl.semaphore_signal(barrier, inc=1, device_id=peer, device_id_type=MESH)

    loads = [
        pltpu.make_async_copy(src, dst, lsem.at[i])
        for i, (src, dst) in enumerate(
            (
                (q_hbm.at[0], qkv.at[0]),
                (k_hbm.at[0], qkv.at[1]),
                (v_hbm.at[0], qkv.at[2]),
                (res_hbm.at[0], residual),
                (mod_hbm, mod),
                (w_out_hbm, w_out.at[0]),
                (w_up_hbm, w_up),
                (w_down_hbm, w_down),
            )
        )
    ]
    for copy in loads[:3]:
        copy.start()

    clips = clip_ref[...].reshape(1, SLOTS).astype(f32)
    first = clips[0:1, 0:1]
    count = jnp.sum(jnp.where(clips < CLIPS, 1.0, 0.0), axis=1, keepdims=True)
    row = lax.broadcasted_iota(jnp.int32, (SLOTS, SLOTS), 0).astype(f32)
    lane = lax.broadcasted_iota(jnp.int32, (SLOTS, SLOTS), 1).astype(f32)
    row_clip = jnp.where(row >= 128, 1.0, 0.0) + jnp.where(row >= 256, 1.0, 0.0)
    step = row_clip - first
    step = jnp.where(step < 0, step + 3, step)
    perm[...] = jnp.where(3 * (row - 128 * row_clip) + step == lane, 1.0, 0.0).astype(bf16)
    rank = lax.broadcasted_iota(jnp.int32, (16, 128), 1).astype(f32)
    for c in range(CLIPS):
        step = c - first
        step = jnp.where(step < 0, step + 3, step)
        bias = jnp.where(3 * rank + step < count, 0.0, NEG_FILL).astype(bf16)
        for h in range(HEADS_HERE):
            stage[3 * h + c, 384:400, :] = bias

    for which in range(3):
        loads[which].wait()
        rows = jnp.dot(perm[...], qkv[which], preferred_element_type=f32).astype(bf16)
        for h in range(HEADS_HERE):
            for c in range(CLIPS):
                stage[3 * h + c, which * 128 : which * 128 + 128, :] = rows[
                    c * 128 : c * 128 + 128, h * 128 : h * 128 + 128
                ]

    pl.semaphore_wait(barrier, len(peers))

    ring = {
        1: remote(stage.at[8, KV], kv9.at[1, KV], rsend.at[1], rrecv.at[1], along(1)),
        7: remote(stage.at[8, KV], kv9.at[7, KV], rsend.at[7], rrecv.at[7], along(7)),
    }
    for copy in ring.values():
        copy.start()
    sends = []
    for t in NEAR_FIRST:
        copy = remote(
            stage.at[(z + t) % Z], buf.at[0, t], zsend.at[t], zrecv.at[t], along(t)
        )
        copy.start()
        sends.append(copy)
    for j, peer in ((1, right), (2, left), (3, across)):
        copy = remote(stage.at[8, pl.ds(0, 128)], q9.at[j], qsend.at[j], qrecv.at[j], peer)
        copy.start()
        sends.append(copy)

    def pass_on(t):
        for j, peer in ((1, right), (2, left)):
            copy = remote(
                buf.at[0, t, KV], buf.at[j, t, KV], ysend.at[j - 1, t], yrecv.at[j - 1, t], peer
            )
            copy.start()
            sends.append(copy)

    buf[0, 0] = stage[z]
    pass_on(0)

    own_rows = pl.ds(pl.multiple_of(side * HALF, HALF), HALF)
    shares = []
    for j, t in ((1, 1), (2, 3), (3, 2)):
        copy = remote(
            w_out_hbm.at[own_rows], w_out.at[j, own_rows], wsend.at[j], wrecv.at[j], over(t)
        )
        copy.start()
        shares.append(copy)

    for copy in loads[3:]:
        copy.start()
    kv9[0] = stage[8]
    q9[0] = stage[8, 0:128, :]
    best_s[...] = jnp.full_like(best_s, NEG_FILL)
    total_s[...] = jnp.zeros_like(total_s)
    accum_s[...] = jnp.zeros_like(accum_s)

    def relay(t, onto, peer):
        ring[t].wait_recv()
        ring[onto] = remote(
            kv9.at[t, KV], kv9.at[onto, KV], rsend.at[onto], rrecv.at[onto], peer
        )
        ring[onto].start()

    owners = owner_ref[...].reshape(1, SLOTS).astype(f32)
    owner_column = jnp.sum(jnp.where(row == lane, owners, 0.0), axis=1, keepdims=True)
    half_start = jnp.where(lane >= HALF, float(HALF), 0.0)
    earlier = (owner_column == owners) & (row < lane) & (row >= half_start)
    ranks = jnp.sum(jnp.where(earlier, 1.0, 0.0), axis=0, keepdims=True)
    owner_y = functools.reduce(
        jnp.add, [jnp.where(owners >= edge, 1.0, 0.0) for edge in (8, 16, 24)]
    )
    target = (owners - 8 * owner_y) * 48 + owner_y * CAP + ranks
    low = side.astype(f32) * HALF
    slot = lane[0:1]
    chosen = (slot < count) & (slot >= low) & (slot < low + HALF)
    target = jnp.where(chosen, target, -1.0)
    by_slot = jnp.where(row == target, 1.0, 0.0).astype(bf16)
    half_perm = jnp.concatenate(
        [perm[pl.ds(pl.multiple_of(c * 128 + side * 64, 64), 64), :] for c in range(CLIPS)], axis=0
    )
    placing[...] = lax.dot_general(
        by_slot, half_perm, (((1,), (1,)), ((), ())), preferred_element_type=f32
    ).astype(bf16)
    from_z = jnp.floor((slot + 0.5) * (1.0 / 48.0))
    within = slot - 48 * from_z
    to_y = jnp.floor((within + 0.5) * (1.0 / CAP))
    repack[...] = jnp.where(
        row == to_y * 96 + from_z * CAP + within - CAP * to_y, 1.0, 0.0
    ).astype(bf16)

    loads[3].wait()
    for k in range(3):
        cols = slice(512 * k, 512 * k + 512)
        mixed[:, cols] = jnp.dot(perm[...], residual[:, cols], preferred_element_type=f32)

    def out_block(problem):
        row = pl.multiple_of((problem % 3) * 128, 128)
        column = pl.multiple_of((problem // 3) * 128, 128)
        return att.at[0, pl.ds(row, 128), pl.ds(column, 128)]

    def returning(t):
        return remote(
            out_stage.at[t], out_block(z), osend.at[t], orecv.at[t], along((Z - t) % Z)
        )

    def from_row(way, t):
        return remote(
            buf.at[0, t, KV], buf.at[1 + way, t, KV],
            ysend.at[way, t], yrecv.at[way, t], (right, left)[way],
        )

    def far_row(t):
        return remote(
            buf.at[1 + t % 2, t, KV], buf.at[3, t, KV],
            ysend.at[2, t], yrecv.at[2, t], (right, left)[t % 2],
        )

    def attend(j, tile):
        rows = pl.ds(pl.multiple_of(tile * 256, 256), 256)
        query = buf[0, pl.ds(2 * tile, 2), 0:128, :].reshape(256, HEAD_DIM)
        best, total, accum = attend_tile(
            query, buf.at[j], best_s[rows, :], total_s[rows, :], accum_s[rows, :]
        )
        best_s[rows, :] = best
        total_s[rows, :] = total
        accum_s[rows, :] = accum
        return total, accum

    def group(j):
        def one(tile, carry):
            attend(j, tile)
            return carry

        lax.fori_loop(0, 4, one, 0, unroll=True)

    for i, t in enumerate(NEAR_FIRST):
        sends[i].wait_recv()
        pass_on(t)
        if i == 1:
            relay(1, 2, along(1))
            relay(7, 6, along(7))
    relay(2, 3, along(1))
    relay(6, 5, along(7))
    for t in (0, 1, 7, 2):
        for way in (0, 1):
            from_row(way, t).wait_recv()
        far_row(t).start()
    group(0)
    relay(3, 4, along(1))
    for t in (6, 3, 5, 4):
        for way in (0, 1):
            from_row(way, t).wait_recv()
        far_row(t).start()
    group(1)
    group(2)

    ring[5].wait_recv()
    ring[4].wait_recv()
    for j in (1, 2, 3):
        sends[6 + j].wait_recv()
    corner = lax.broadcasted_iota(jnp.int32, (128, 128), 0) == lax.broadcasted_iota(
        jnp.int32, (128, 128), 1
    )

    def ninth(tile, carry):
        query = q9[pl.ds(2 * tile, 2)].reshape(256, HEAD_DIM)
        zero = jnp.zeros((256, HEAD_DIM), f32)
        best, total, accum = attend_tile(query, kv9, zero + NEG_FILL, zero, zero)
        total = jnp.sum(total, axis=1, keepdims=True)
        part_out[pl.ds(2 * tile, 2)] = (accum / total).astype(bf16).reshape(2, 128, 128)
        for i in range(2):
            rows = slice(128 * i, 128 * i + 128)
            for at, column in ((0, best[rows, 0:1]), (8, total[rows])):
                line = jnp.sum(jnp.where(corner, column, 0.0), axis=0, keepdims=True)
                stat_out[2 * tile + i, at : at + 8, :] = jnp.broadcast_to(line, (8, 128))
        return carry

    lax.fori_loop(0, 2, ninth, 0, unroll=True)
    parts = []
    for j, onto, peer in ((1, 2, left), (2, 1, right), (3, 3, across)):
        for copy in (
            remote(part_out.at[j], part_in.at[onto], psend.at[j], precv.at[onto], peer),
            remote(stat_out.at[j], stat_in.at[onto], ssend.at[j], srecv.at[onto], peer),
        ):
            copy.start()
            parts.append(copy)

    for t in range(Z):
        far_row(t).wait()

    def finish_tile(tile, carry):
        total, accum = attend(3, tile)
        result = accum / jnp.sum(total, axis=1, keepdims=True)
        out_stage[pl.ds(2 * tile, 2)] = result.astype(bf16).reshape(2, 128, 128)

        @pl.when(tile > 0)
        def _():
            returning(2 * tile).start()

        returning(2 * tile + 1).start()
        return carry

    lax.fori_loop(0, 4, finish_tile, 0, unroll=True)
    own_block = pltpu.make_async_copy(out_stage.at[0], out_block(z), osend.at[0])
    own_block.start()

    swaps = []
    for j, copy in enumerate(shares, 1):
        copy.wait()
        swap = remote(
            w_out.at[j, own_rows], w_out.at[j, own_rows], csend.at[j], crecv.at[j], other_core
        )
        swap.start()
        swaps.append(swap)

    for copy in parts:
        copy.wait()
    lines = [stat_out.at[0], stat_in.at[1], stat_in.at[2], stat_in.at[3]]
    pieces = [part_out.at[0], part_in.at[1], part_in.at[2], part_in.at[3]]
    bests = [line[0:1, :] for line in lines]
    top = functools.reduce(jnp.maximum, bests)
    weights = [
        jnp.exp2((best - top) * EXP2_SCALE) * line[8:9, :] for best, line in zip(bests, lines)
    ]
    total = functools.reduce(jnp.add, weights)
    accum = functools.reduce(
        jnp.add,
        [
            jnp.sum(jnp.where(corner, weight / total, 0.0), axis=1, keepdims=True)
            * piece[...].astype(f32)
            for weight, piece in zip(weights, pieces)
        ],
    )
    att[0, 256:384, 256:384] = accum.astype(bf16)

    own_block.wait()
    for t in range(1, Z):
        remote(
            out_stage.at[t], out_block((z + t) % Z), osend.at[t], orecv.at[t], along(Z - t)
        ).wait_recv()

    gathers = {}

    def hop(src, slot, part, peer):
        rows = (TOP, LOW)[part]
        copy = remote(
            att.at[src, rows], att.at[slot, rows], asend.at[slot, part], arecv.at[slot, part], peer
        )
        copy.start()
        gathers[slot, part] = copy

    hop(0, 1, 0, over(1))
    hop(0, 2, 1, over(3))
    hop(0, 1, 1, over(1))
    hop(0, 2, 0, over(3))

    for copy in loads[4:6]:
        copy.wait()
    for copy in swaps:
        copy.wait()

    def project(slot):
        rows = att[slot]

        def one(k, carry):
            cols = pl.ds(pl.multiple_of(k * 512, 512), 512)
            term = jnp.dot(rows, w_out[slot, :, cols], preferred_element_type=f32)
            for c in range(CLIPS):
                part = slice(128 * c, 128 * c + 128)
                mixed[part, cols] += mod[c, 0:1, cols] * term[part]
            return carry

        lax.fori_loop(0, 3, one, 0, unroll=True)

    gathers[1, 0].wait_recv()
    hop(1, 3, 0, over(1))
    gathers[2, 1].wait_recv()
    hop(2, 3, 1, over(3))
    project(0)
    gathers[1, 1].wait_recv()
    project(1)
    gathers[2, 0].wait_recv()
    project(2)
    gathers[3, 0].wait_recv()
    gathers[3, 1].wait_recv()
    project(3)

    def normalise(k, carry):
        for c in range(CLIPS):
            rows = pl.ds(pl.multiple_of(c * 128 + k * 32, 32), 32)
            value = mixed[rows, :]
            centre = value - jnp.mean(value, axis=1, keepdims=True)
            spread = jnp.mean(centre * centre, axis=1, keepdims=True)
            scaled = centre * lax.rsqrt(spread + 1e-06) * (1.0 + mod[c, 2:3, :]) + mod[c, 1:2, :]
            to = pl.multiple_of((k // 2) * HALF + c * 64 + (k % 2) * 32, 32)
            normed[pl.ds(to, 32), :] = scaled.astype(bf16)
        return carry

    lax.fori_loop(0, 4, normalise, 0, unroll=True)

    loads[6].wait()

    def expand(k, carry):
        cols = pl.ds(pl.multiple_of(k * 512, 512), 512)
        value = jnp.dot(normed[...], w_up[:, cols], preferred_element_type=f32)
        hidden[:, cols] = jax.nn.gelu(value, approximate=True).astype(bf16)
        return carry

    lax.fori_loop(0, 3, expand, 0, unroll=True)

    loads[7].wait()

    def contract(t):
        cols = pl.ds(pl.multiple_of(((blk + t) % X) * SLOTS, SLOTS), SLOTS)
        return jnp.dot(hidden[...], w_down[:, cols], preferred_element_type=f32)

    passing, finals = {}, {}

    def chunk(k):
        return slice(128 * k, 128 * k + 128)

    def give_far(k):
        for way, rows in ((0, TOP), (1, LOW)):
            passing[way, k] = remote(
                far.at[k, rows], transit.at[way, k],
                tsend.at[way, k], trecv.at[way, k], over((1, 3)[way]),
            )
            passing[way, k].start()

    def near_terms(way):
        terms = contract((1, 3)[way])
        low = (HALF, 0)[way]
        for k in range(3):
            near[way, k] = terms[:, chunk(k)]
            ready[1 + way, k] = terms[low : low + HALF, chunk(k)].astype(bf16)

    def deliver(which, k):
        finals[which, k] = remote(
            ready.at[which, k], final.at[side, which // 2, k],
            fsend.at[which, k], frecv.at[side, which // 2, k],
            {**over((1, 1, 3, 3)[which]), "cfg": which % 2},
        )
        finals[which, k].start()

    def merge(k):
        for way, which, rows in ((0, 0, TOP), (1, 3, LOW)):
            passing[way, k].wait_recv()
            ready[which, k] = (near[way, k, rows, :] + transit[way, k].astype(f32)).astype(bf16)
            deliver(which, k)

    trips, last = [], []
    here = pl.ds(pl.multiple_of(z * 48, 16), 48)

    def send_rows(k):
        cols = pl.ds(pl.multiple_of(blk * SLOTS + 128 * k, 128), 128)
        for source in range(2):
            for way in range(2):
                remote(
                    ready.at[way, k], final.at[source, way, k],
                    fsend.at[way, k], frecv.at[source, way, k], over(1),
                ).wait_recv()
        guided = []
        for c in range(CLIPS):
            rows = slice(64 * c, 64 * c + 64)
            cond, uncond = (
                (
                    base[source, rows, chunk(k)]
                    + mod[c, 3:4, cols]
                    * (final[source, 0, k, rows].astype(f32) + final[source, 1, k, rows].astype(f32))
                )
                .astype(bf16)
                .astype(f32)
                for source in range(2)
            )
            guided.append((uncond + guide_ref[c] * (cond - uncond)).astype(bf16))
        guided = jnp.concatenate(guided, axis=0)
        going[k] = jnp.dot(placing[...], guided, preferred_element_type=f32).astype(bf16)
        for t in NEAR_FIRST[::-1]:
            there = pl.ds(pl.multiple_of(((z + t) % Z) * 48, 16), 48)
            copy = remote(
                going.at[k, there], landed.at[k, here], gsend.at[k, t], grecv.at[k, t], along(t)
            )
            copy.start()
            trips.append(copy)
        landed[k, here, :] = going[k, here, :]

    row_here = pl.ds(pl.multiple_of(y * 96, 96), 96)

    def turn_rows(k):
        cols = pl.ds(128 * k, 128)
        for copy in trips[7 * k : 7 * k + 7]:
            copy.wait_recv()
        turned[k] = jnp.dot(repack[...], landed[k], preferred_element_type=f32).astype(bf16)
        for t in (1, 3, 2):
            there = pl.ds(pl.multiple_of(((y + t) % Y) * 96, 96), 96)
            copy = remote(
                turned.at[k, there], out_ref.at[0, row_here, cols],
                hsend.at[k, t], hrecv.at[k, t], up(t),
            )
            copy.start()
            last.append(copy)
        out_ref[0, row_here, 128 * k : 128 * k + 128] = turned[k, row_here, :]

    far_terms = contract(2).astype(bf16)
    for k in range(3):
        far[k] = far_terms[:, chunk(k)]
    give_far(0)
    give_far(1)
    for way in range(2):
        near_terms(way)
        deliver(1 + way, 0)
    own = contract(0)
    own_cols = pl.ds(pl.multiple_of(blk * SLOTS, SLOTS), SLOTS)
    for half in range(2):
        for c in range(CLIPS):
            at, start = c * 64, c * 128 + half * 64
            mine[half, at : at + 64, :] = (
                mixed[start : start + 64, own_cols]
                + mod[c, 3:4, own_cols] * own[half * HALF + at : half * HALF + at + 64]
            )
    exchange = remote(mine.at[1 - side], base.at[side], esend.at[0], erecv.at[0], other_core)
    exchange.start()
    base[side] = mine[side]

    merge(0)
    give_far(2)
    deliver(1, 1)
    deliver(2, 1)
    merge(1)
    deliver(1, 2)
    deliver(2, 2)
    remote(mine.at[side], base.at[1 - side], esend.at[0], erecv.at[0], other_core).wait_recv()
    send_rows(0)
    merge(2)
    send_rows(1)
    send_rows(2)
    turn_rows(0)
    turn_rows(1)
    turn_rows(2)
    for copy in last:
        copy.wait()

    for t in range(1, Z):
        returning(t).wait_send()
    for copy in [
        *sends, *ring.values(), *gathers.values(), *passing.values(), *finals.values(),
        exchange, *trips,
    ]:
        copy.wait_send()


def block(clips, owners, guide_scale, *arrays):
    dma = pltpu.SemaphoreType.DMA
    vmem = pltpu.VMEM
    f32, bf16 = jnp.float32, jnp.bfloat16
    return pl.pallas_call(
        block_kernel,
        out_shape=jax.ShapeDtypeStruct((1, SLOTS, SLOTS), bf16),
        in_specs=[
            pl.BlockSpec(memory_space=vmem),
            pl.BlockSpec(memory_space=vmem),
            pl.BlockSpec(memory_space=pltpu.SMEM),
            *[pl.BlockSpec(memory_space=pl.ANY)] * 8,
        ],
        out_specs=pl.BlockSpec(memory_space=vmem),
        scratch_shapes=[
            vmem((3, SLOTS, SLOTS), bf16),
            vmem((SLOTS, SLOTS), bf16),
            vmem((9, MSG, 128), bf16),
            vmem((4, Z, MSG, 128), bf16),
            vmem((Z, MSG, 128), bf16),
            vmem((4, 128, 128), bf16),
            vmem((4, 128, 128), bf16),
            vmem((4, 128, 128), bf16),
            vmem((4, 16, 128), f32),
            vmem((4, 16, 128), f32),
            vmem((1024, 128), f32),
            vmem((1024, 128), f32),
            vmem((1024, 128), f32),
            vmem((Z, 128, 128), bf16),
            vmem((4, SLOTS, SLOTS), bf16),
            vmem((4, SLOTS, D), bf16),
            vmem((D, D), bf16),
            vmem((D, D), bf16),
            vmem((SLOTS, D), bf16),
            vmem((CLIPS, 4, D), f32),
            vmem((SLOTS, D), f32),
            vmem((SLOTS, D), bf16),
            vmem((SLOTS, D), bf16),
            vmem((3, SLOTS, 128), bf16),
            vmem((2, 3, SLOTS, 128), f32),
            vmem((4, 3, HALF, 128), bf16),
            vmem((2, 3, HALF, 128), bf16),
            vmem((2, 2, 3, HALF, 128), bf16),
            vmem((2, HALF, SLOTS), f32),
            vmem((2, HALF, SLOTS), f32),
            vmem((SLOTS, HALF), bf16),
            vmem((SLOTS, SLOTS), bf16),
            vmem((3, SLOTS, 128), bf16),
            vmem((3, SLOTS, 128), bf16),
            vmem((3, SLOTS, 128), bf16),
            dma((8,)),
            *[dma((Z,))] * 4,
            *[dma((3, Z))] * 2,
            *[dma((4,))] * 6,
            *[dma((Z,))] * 2,
            *[dma((4,))] * 4,
            *[dma((4, 2))] * 2,
            *[dma((2, 3))] * 2,
            dma((4, 3)),
            dma((2, 2, 3)),
            *[dma((1,))] * 2,
            *[dma((3, Z))] * 2,
            *[dma((3, Y))] * 2,
        ],
        compiler_params=pltpu.CompilerParams(
            collective_id=0, has_side_effects=True, vmem_limit_bytes=56 * 2**20
        ),
        name="guided_block",
    )(clips, owners, guide_scale, *arrays)


def shards(
    queries, keys, values, residual, w_out, w_up, w_down, modulation, guide_scale, slot_clip, owner
):
    return block(
        slot_clip,
        owner.reshape(SLOTS),
        guide_scale,
        queries,
        keys,
        values,
        residual,
        modulation,
        w_out,
        w_up,
        w_down,
    )


def solution(mesh):
    placed = (
        P("cfg", "seq", "blk"),
        P("cfg", "seq", "blk"),
        P("cfg", "seq", "blk"),
        P("cfg", "seq", None),
        P("blk", None),
        P(None, "blk"),
        P("blk", None),
        P(),
        P(),
        P("seq"),
        P("seq", None),
    )
    return jax.shard_map(
        shards, mesh=mesh, in_specs=placed, out_specs=P("cfg", "seq", "blk"), check_vma=False
    )
```

```python
import functools
import math

import jax
import jax.numpy as jnp
from jax import lax
from jax.experimental import pallas as pl
from jax.experimental.pallas import tpu as pltpu
from jax.sharding import PartitionSpec as P

D = 1536
HEAD_DIM = 128
CLIPS = 3
HEADS_HERE = 3
GROUP = 128
Y, Z = 4, 8
MSG = 400
KV = pl.ds(128, 272)
NEG_FILL = -1e30
EXP2_SCALE = math.log2(math.e) / math.sqrt(HEAD_DIM)
MESH = pl.DeviceIdType.MESH
NEAR_FIRST = (1, 7, 2, 6, 3, 5, 4)
X = 4
SLOTS = 384
HALF = 192
CAP = 12
TOP, LOW = pl.ds(0, HALF), pl.ds(HALF, HALF)


def remote(src, dst, send, recv, peer):
    return pltpu.make_async_remote_copy(
        src_ref=src,
        dst_ref=dst,
        send_sem=send,
        recv_sem=recv,
        device_id=peer,
        device_id_type=MESH,
    )


def attend_tile(query, kv, best, total, accum):
    count = kv.shape[0]
    keys = kv[:, 128:256, :].reshape(count * GROUP, HEAD_DIM)
    scores = lax.dot_general(
        query, keys, (((1,), (1,)), ((), ())), preferred_element_type=jnp.float32
    )
    pieces = []
    for i in range(count):
        bias = kv[i, 384:400, :].astype(jnp.float32)[0:1]
        pieces.append(scores[:, i * GROUP : (i + 1) * GROUP] + bias)
    peak = functools.reduce(jnp.maximum, pieces)
    new_best = jnp.maximum(best, jnp.max(peak, axis=1, keepdims=True))
    probs = [jnp.exp2((piece - new_best) * EXP2_SCALE) for piece in pieces]
    fade = jnp.exp2((best - new_best) * EXP2_SCALE)
    total = total * fade + functools.reduce(jnp.add, probs)
    weights = jnp.concatenate([prob.astype(jnp.bfloat16) for prob in probs], axis=1)
    values = kv[:, 256:384, :].reshape(count * GROUP, HEAD_DIM)
    accum = accum * fade + jnp.dot(weights, values, preferred_element_type=jnp.float32)
    return new_best, total, accum


def block_kernel(
    clip_ref,
    owner_ref,
    guide_ref,
    q_hbm,
    k_hbm,
    v_hbm,
    res_hbm,
    mod_hbm,
    w_out_hbm,
    w_up_hbm,
    w_down_hbm,
    out_ref,
    qkv,
    perm,
    stage,
    buf,
    kv9,
    q9,
    part_out,
    part_in,
    stat_out,
    stat_in,
    best_s,
    total_s,
    accum_s,
    out_stage,
    att,
    w_out,
    w_up,
    w_down,
    residual,
    mod,
    mixed,
    normed,
    hidden,
    far,
    near,
    ready,
    transit,
    final,
    mine,
    base,
    placing,
    repack,
    going,
    landed,
    turned,
    lsem,
    zsend,
    zrecv,
    rsend,
    rrecv,
    ysend,
    yrecv,
    qsend,
    qrecv,
    psend,
    precv,
    ssend,
    srecv,
    osend,
    orecv,
    wsend,
    wrecv,
    csend,
    crecv,
    asend,
    arecv,
    tsend,
    trecv,
    fsend,
    frecv,
    esend,
    erecv,
    gsend,
    grecv,
    hsend,
    hrecv,
):
    f32, bf16 = jnp.float32, jnp.bfloat16
    me = lax.axis_index("seq")
    side = lax.axis_index("cfg")
    blk = lax.axis_index("blk")
    y, z = me // Z, me % Z

    def up(t):
        return {"seq": ((y + t) % Y) * Z + z}

    def along(t):
        return {"seq": y * Z + (z + t) % Z}

    def over(t):
        return {"blk": (blk + t) % X}

    right, left, across = up(1), up(3), up(2)
    other_core = {"cfg": 1 - side}

    barrier = pltpu.get_barrier_semaphore()
    peers = [along(t) for t in range(1, Z)] + [up(t) for t in range(1, Y)]
    peers += [over(t) for t in range(1, X)] + [other_core]
    peers += [{**over(t), **other_core} for t in (1, 3)]
    for peer in peers:
        pl.semaphore_signal(barrier, inc=1, device_id=peer, device_id_type=MESH)

    loads = [
        pltpu.make_async_copy(src, dst, lsem.at[i])
        for i, (src, dst) in enumerate(
            (
                (q_hbm.at[0], qkv.at[0]),
                (k_hbm.at[0], qkv.at[1]),
                (v_hbm.at[0], qkv.at[2]),
                (res_hbm.at[0], residual),
                (mod_hbm, mod),
                (w_out_hbm, w_out.at[0]),
                (w_up_hbm, w_up),
                (w_down_hbm, w_down),
            )
        )
    ]
    for copy in loads[:3]:
        copy.start()

    clips = clip_ref[...].reshape(1, SLOTS).astype(f32)
    first = clips[0:1, 0:1]
    count = jnp.sum(jnp.where(clips < CLIPS, 1.0, 0.0), axis=1, keepdims=True)
    row = lax.broadcasted_iota(jnp.int32, (SLOTS, SLOTS), 0).astype(f32)
    lane = lax.broadcasted_iota(jnp.int32, (SLOTS, SLOTS), 1).astype(f32)
    row_clip = jnp.where(row >= 128, 1.0, 0.0) + jnp.where(row >= 256, 1.0, 0.0)
    step = row_clip - first
    step = jnp.where(step < 0, step + 3, step)
    perm[...] = jnp.where(3 * (row - 128 * row_clip) + step == lane, 1.0, 0.0).astype(bf16)
    rank = lax.broadcasted_iota(jnp.int32, (16, 128), 1).astype(f32)
    for c in range(CLIPS):
        step = c - first
        step = jnp.where(step < 0, step + 3, step)
        bias = jnp.where(3 * rank + step < count, 0.0, NEG_FILL).astype(bf16)
        for h in range(HEADS_HERE):
            stage[3 * h + c, 384:400, :] = bias

    for which in range(3):
        loads[which].wait()
        rows = jnp.dot(perm[...], qkv[which], preferred_element_type=f32).astype(bf16)
        for h in range(HEADS_HERE):
            for c in range(CLIPS):
                stage[3 * h + c, which * 128 : which * 128 + 128, :] = rows[
                    c * 128 : c * 128 + 128, h * 128 : h * 128 + 128
                ]

    pl.semaphore_wait(barrier, len(peers))

    ring = {
        1: remote(stage.at[8, KV], kv9.at[1, KV], rsend.at[1], rrecv.at[1], along(1)),
        7: remote(stage.at[8, KV], kv9.at[7, KV], rsend.at[7], rrecv.at[7], along(7)),
    }
    for copy in ring.values():
        copy.start()
    sends = []
    for t in NEAR_FIRST:
        copy = remote(
            stage.at[(z + t) % Z], buf.at[0, t], zsend.at[t], zrecv.at[t], along(t)
        )
        copy.start()
        sends.append(copy)
    for j, peer in ((1, right), (2, left), (3, across)):
        copy = remote(stage.at[8, pl.ds(0, 128)], q9.at[j], qsend.at[j], qrecv.at[j], peer)
        copy.start()
        sends.append(copy)

    def pass_on(t):
        for j, peer in ((1, right), (2, left)):
            copy = remote(
                buf.at[0, t, KV], buf.at[j, t, KV], ysend.at[j - 1, t], yrecv.at[j - 1, t], peer
            )
            copy.start()
            sends.append(copy)

    buf[0, 0] = stage[z]
    pass_on(0)

    own_rows = pl.ds(pl.multiple_of(side * HALF, HALF), HALF)
    shares = []
    for j, t in ((1, 1), (2, 3), (3, 2)):
        copy = remote(
            w_out_hbm.at[own_rows], w_out.at[j, own_rows], wsend.at[j], wrecv.at[j], over(t)
        )
        copy.start()
        shares.append(copy)

    for copy in loads[3:]:
        copy.start()
    kv9[0] = stage[8]
    q9[0] = stage[8, 0:128, :]
    best_s[...] = jnp.full_like(best_s, NEG_FILL)
    total_s[...] = jnp.zeros_like(total_s)
    accum_s[...] = jnp.zeros_like(accum_s)

    def relay(t, onto, peer):
        ring[t].wait_recv()
        ring[onto] = remote(
            kv9.at[t, KV], kv9.at[onto, KV], rsend.at[onto], rrecv.at[onto], peer
        )
        ring[onto].start()

    owners = owner_ref[...].reshape(1, SLOTS).astype(f32)
    owner_column = jnp.sum(jnp.where(row == lane, owners, 0.0), axis=1, keepdims=True)
    half_start = jnp.where(lane >= HALF, float(HALF), 0.0)
    earlier = (owner_column == owners) & (row < lane) & (row >= half_start)
    ranks = jnp.sum(jnp.where(earlier, 1.0, 0.0), axis=0, keepdims=True)
    owner_y = functools.reduce(
        jnp.add, [jnp.where(owners >= edge, 1.0, 0.0) for edge in (8, 16, 24)]
    )
    target = (owners - 8 * owner_y) * 48 + owner_y * CAP + ranks
    low = side.astype(f32) * HALF
    slot = lane[0:1]
    chosen = (slot < count) & (slot >= low) & (slot < low + HALF)
    target = jnp.where(chosen, target, -1.0)
    by_slot = jnp.where(row == target, 1.0, 0.0).astype(bf16)
    half_perm = jnp.concatenate(
        [perm[pl.ds(pl.multiple_of(c * 128 + side * 64, 64), 64), :] for c in range(CLIPS)], axis=0
    )
    placing[...] = lax.dot_general(
        by_slot, half_perm, (((1,), (1,)), ((), ())), preferred_element_type=f32
    ).astype(bf16)
    from_z = jnp.floor((slot + 0.5) * (1.0 / 48.0))
    within = slot - 48 * from_z
    to_y = jnp.floor((within + 0.5) * (1.0 / CAP))
    repack[...] = jnp.where(
        row == to_y * 96 + from_z * CAP + within - CAP * to_y, 1.0, 0.0
    ).astype(bf16)

    loads[3].wait()
    for k in range(3):
        cols = slice(512 * k, 512 * k + 512)
        mixed[:, cols] = jnp.dot(perm[...], residual[:, cols], preferred_element_type=f32)

    def out_block(problem):
        row = pl.multiple_of((problem % 3) * 128, 128)
        column = pl.multiple_of((problem // 3) * 128, 128)
        return att.at[0, pl.ds(row, 128), pl.ds(column, 128)]

    def returning(t):
        return remote(
            out_stage.at[t], out_block(z), osend.at[t], orecv.at[t], along((Z - t) % Z)
        )

    def from_row(way, t):
        return remote(
            buf.at[0, t, KV], buf.at[1 + way, t, KV],
            ysend.at[way, t], yrecv.at[way, t], (right, left)[way],
        )

    def far_row(t):
        return remote(
            buf.at[1 + t % 2, t, KV], buf.at[3, t, KV],
            ysend.at[2, t], yrecv.at[2, t], (right, left)[t % 2],
        )

    def attend(j, tile):
        rows = pl.ds(pl.multiple_of(tile * 256, 256), 256)
        query = buf[0, pl.ds(2 * tile, 2), 0:128, :].reshape(256, HEAD_DIM)
        best, total, accum = attend_tile(
            query, buf.at[j], best_s[rows, :], total_s[rows, :], accum_s[rows, :]
        )
        best_s[rows, :] = best
        total_s[rows, :] = total
        accum_s[rows, :] = accum
        return total, accum

    def group(j):
        def one(tile, carry):
            attend(j, tile)
            return carry

        lax.fori_loop(0, 4, one, 0, unroll=True)

    for i, t in enumerate(NEAR_FIRST):
        sends[i].wait_recv()
        pass_on(t)
        if i == 1:
            relay(1, 2, along(1))
            relay(7, 6, along(7))
    relay(2, 3, along(1))
    relay(6, 5, along(7))
    for t in (0, 1, 7, 2):
        for way in (0, 1):
            from_row(way, t).wait_recv()
        far_row(t).start()
    group(0)
    relay(3, 4, along(1))
    for t in (6, 3, 5, 4):
        for way in (0, 1):
            from_row(way, t).wait_recv()
        far_row(t).start()
    group(1)
    group(2)

    ring[5].wait_recv()
    ring[4].wait_recv()
    for j in (1, 2, 3):
        sends[6 + j].wait_recv()
    corner = lax.broadcasted_iota(jnp.int32, (128, 128), 0) == lax.broadcasted_iota(
        jnp.int32, (128, 128), 1
    )

    def ninth(tile, carry):
        query = q9[pl.ds(2 * tile, 2)].reshape(256, HEAD_DIM)
        zero = jnp.zeros((256, HEAD_DIM), f32)
        best, total, accum = attend_tile(query, kv9, zero + NEG_FILL, zero, zero)
        total = jnp.sum(total, axis=1, keepdims=True)
        part_out[pl.ds(2 * tile, 2)] = (accum / total).astype(bf16).reshape(2, 128, 128)
        for i in range(2):
            rows = slice(128 * i, 128 * i + 128)
            for at, column in ((0, best[rows, 0:1]), (8, total[rows])):
                line = jnp.sum(jnp.where(corner, column, 0.0), axis=0, keepdims=True)
                stat_out[2 * tile + i, at : at + 8, :] = jnp.broadcast_to(line, (8, 128))
        return carry

    lax.fori_loop(0, 2, ninth, 0, unroll=True)
    parts = []
    for j, onto, peer in ((1, 2, left), (2, 1, right), (3, 3, across)):
        for copy in (
            remote(part_out.at[j], part_in.at[onto], psend.at[j], precv.at[onto], peer),
            remote(stat_out.at[j], stat_in.at[onto], ssend.at[j], srecv.at[onto], peer),
        ):
            copy.start()
            parts.append(copy)

    for t in range(Z):
        far_row(t).wait()

    for tile in (2, 1, 3, 0):
        total, accum = attend(3, tile)
        result = accum / jnp.sum(total, axis=1, keepdims=True)
        out_stage[pl.ds(2 * tile, 2)] = result.astype(bf16).reshape(2, 128, 128)

        if tile:
            returning(2 * tile).start()
        returning(2 * tile + 1).start()
    own_block = pltpu.make_async_copy(out_stage.at[0], out_block(z), osend.at[0])
    own_block.start()

    swaps = []
    for j, copy in enumerate(shares, 1):
        copy.wait()
        swap = remote(
            w_out.at[j, own_rows], w_out.at[j, own_rows], csend.at[j], crecv.at[j], other_core
        )
        swap.start()
        swaps.append(swap)

    for copy in parts:
        copy.wait()
    lines = [stat_out.at[0], stat_in.at[1], stat_in.at[2], stat_in.at[3]]
    pieces = [part_out.at[0], part_in.at[1], part_in.at[2], part_in.at[3]]
    bests = [line[0:1, :] for line in lines]
    top = functools.reduce(jnp.maximum, bests)
    weights = [
        jnp.exp2((best - top) * EXP2_SCALE) * line[8:9, :] for best, line in zip(bests, lines)
    ]
    total = functools.reduce(jnp.add, weights)
    accum = functools.reduce(
        jnp.add,
        [
            jnp.sum(jnp.where(corner, weight / total, 0.0), axis=1, keepdims=True)
            * piece[...].astype(f32)
            for weight, piece in zip(weights, pieces)
        ],
    )
    att[0, 256:384, 256:384] = accum.astype(bf16)

    own_block.wait()
    for t in range(1, Z):
        remote(
            out_stage.at[t], out_block((z + t) % Z), osend.at[t], orecv.at[t], along(Z - t)
        ).wait_recv()

    gathers = {}

    def hop(src, slot, part, peer):
        rows = (TOP, LOW)[part]
        copy = remote(
            att.at[src, rows], att.at[slot, rows], asend.at[slot, part], arecv.at[slot, part], peer
        )
        copy.start()
        gathers[slot, part] = copy

    hop(0, 1, 0, over(1))
    hop(0, 2, 1, over(3))
    hop(0, 1, 1, over(1))
    hop(0, 2, 0, over(3))

    for copy in loads[4:6]:
        copy.wait()
    for copy in swaps:
        copy.wait()

    def project(slot):
        rows = att[slot]

        def one(k, carry):
            cols = pl.ds(pl.multiple_of(k * 512, 512), 512)
            term = jnp.dot(rows, w_out[slot, :, cols], preferred_element_type=f32)
            for c in range(CLIPS):
                part = slice(128 * c, 128 * c + 128)
                mixed[part, cols] += mod[c, 0:1, cols] * term[part]
            return carry

        lax.fori_loop(0, 3, one, 0, unroll=True)

    gathers[1, 0].wait_recv()
    hop(1, 3, 0, over(1))
    gathers[2, 1].wait_recv()
    hop(2, 3, 1, over(3))
    project(0)
    gathers[1, 1].wait_recv()
    project(1)
    gathers[2, 0].wait_recv()
    project(2)
    gathers[3, 0].wait_recv()
    gathers[3, 1].wait_recv()
    project(3)

    def normalise(k, carry):
        for c in range(CLIPS):
            rows = pl.ds(pl.multiple_of(c * 128 + k * 32, 32), 32)
            value = mixed[rows, :]
            centre = value - jnp.mean(value, axis=1, keepdims=True)
            spread = jnp.mean(centre * centre, axis=1, keepdims=True)
            scaled = centre * lax.rsqrt(spread + 1e-06) * (1.0 + mod[c, 2:3, :]) + mod[c, 1:2, :]
            to = pl.multiple_of((k // 2) * HALF + c * 64 + (k % 2) * 32, 32)
            normed[pl.ds(to, 32), :] = scaled.astype(bf16)
        return carry

    lax.fori_loop(0, 4, normalise, 0, unroll=True)

    loads[6].wait()

    def expand(k, carry):
        cols = pl.ds(pl.multiple_of(k * 512, 512), 512)
        value = jnp.dot(normed[...], w_up[:, cols], preferred_element_type=f32)
        hidden[:, cols] = jax.nn.gelu(value, approximate=True).astype(bf16)
        return carry

    lax.fori_loop(0, 3, expand, 0, unroll=True)

    loads[7].wait()

    def contract(t):
        cols = pl.ds(pl.multiple_of(((blk + t) % X) * SLOTS, SLOTS), SLOTS)
        return jnp.dot(hidden[...], w_down[:, cols], preferred_element_type=f32)

    passing, finals = {}, {}

    def chunk(k):
        return slice(128 * k, 128 * k + 128)

    def give_far(k):
        for way, rows in ((0, TOP), (1, LOW)):
            passing[way, k] = remote(
                far.at[k, rows], transit.at[way, k],
                tsend.at[way, k], trecv.at[way, k], over((1, 3)[way]),
            )
            passing[way, k].start()

    def near_terms(way):
        terms = contract((1, 3)[way])
        low = (HALF, 0)[way]
        for k in range(3):
            near[way, k] = terms[:, chunk(k)]
            ready[1 + way, k] = terms[low : low + HALF, chunk(k)].astype(bf16)

    def deliver(which, k):
        finals[which, k] = remote(
            ready.at[which, k], final.at[side, which // 2, k],
            fsend.at[which, k], frecv.at[side, which // 2, k],
            {**over((1, 1, 3, 3)[which]), "cfg": which % 2},
        )
        finals[which, k].start()

    def merge(k):
        for way, which, rows in ((0, 0, TOP), (1, 3, LOW)):
            passing[way, k].wait_recv()
            ready[which, k] = (near[way, k, rows, :] + transit[way, k].astype(f32)).astype(bf16)
            deliver(which, k)

    trips, last = [], []
    here = pl.ds(pl.multiple_of(z * 48, 16), 48)

    def send_rows(k):
        cols = pl.ds(pl.multiple_of(blk * SLOTS + 128 * k, 128), 128)
        for source in range(2):
            for way in range(2):
                remote(
                    ready.at[way, k], final.at[source, way, k],
                    fsend.at[way, k], frecv.at[source, way, k], over(1),
                ).wait_recv()
        guided = []
        for c in range(CLIPS):
            rows = slice(64 * c, 64 * c + 64)
            cond, uncond = (
                (
                    base[source, rows, chunk(k)]
                    + mod[c, 3:4, cols]
                    * (final[source, 0, k, rows].astype(f32) + final[source, 1, k, rows].astype(f32))
                )
                .astype(bf16)
                .astype(f32)
                for source in range(2)
            )
            guided.append((uncond + guide_ref[c] * (cond - uncond)).astype(bf16))
        guided = jnp.concatenate(guided, axis=0)
        going[k] = jnp.dot(placing[...], guided, preferred_element_type=f32).astype(bf16)
        for t in NEAR_FIRST[::-1]:
            there = pl.ds(pl.multiple_of(((z + t) % Z) * 48, 16), 48)
            copy = remote(
                going.at[k, there], landed.at[k, here], gsend.at[k, t], grecv.at[k, t], along(t)
            )
            copy.start()
            trips.append(copy)
        landed[k, here, :] = going[k, here, :]

    row_here = pl.ds(pl.multiple_of(y * 96, 96), 96)

    def turn_rows(k):
        cols = pl.ds(128 * k, 128)
        for copy in trips[7 * k : 7 * k + 7]:
            copy.wait_recv()
        turned[k] = jnp.dot(repack[...], landed[k], preferred_element_type=f32).astype(bf16)
        for t in (1, 3, 2):
            there = pl.ds(pl.multiple_of(((y + t) % Y) * 96, 96), 96)
            copy = remote(
                turned.at[k, there], out_ref.at[0, row_here, cols],
                hsend.at[k, t], hrecv.at[k, t], up(t),
            )
            copy.start()
            last.append(copy)
        out_ref[0, row_here, 128 * k : 128 * k + 128] = turned[k, row_here, :]

    far_terms = contract(2).astype(bf16)
    for k in range(3):
        far[k] = far_terms[:, chunk(k)]
    give_far(0)
    give_far(1)
    for way in range(2):
        near_terms(way)
        deliver(1 + way, 0)
    merge(0)
    give_far(2)
    own = contract(0)
    own_cols = pl.ds(pl.multiple_of(blk * SLOTS, SLOTS), SLOTS)
    for half in range(2):
        for c in range(CLIPS):
            at, start = c * 64, c * 128 + half * 64
            mine[half, at : at + 64, :] = (
                mixed[start : start + 64, own_cols]
                + mod[c, 3:4, own_cols] * own[half * HALF + at : half * HALF + at + 64]
            )
    exchange = remote(mine.at[1 - side], base.at[side], esend.at[0], erecv.at[0], other_core)
    exchange.start()
    base[side] = mine[side]

    deliver(1, 1)
    deliver(2, 1)
    merge(1)
    deliver(1, 2)
    deliver(2, 2)
    remote(mine.at[side], base.at[1 - side], esend.at[0], erecv.at[0], other_core).wait_recv()
    send_rows(0)
    merge(2)
    send_rows(1)
    send_rows(2)
    turn_rows(0)
    turn_rows(1)
    turn_rows(2)
    for copy in last:
        copy.wait()

    for t in range(1, Z):
        returning(t).wait_send()
    for copy in [
        *sends, *ring.values(), *gathers.values(), *passing.values(), *finals.values(),
        exchange, *trips,
    ]:
        copy.wait_send()


def block(clips, owners, guide_scale, *arrays):
    dma = pltpu.SemaphoreType.DMA
    vmem = pltpu.VMEM
    f32, bf16 = jnp.float32, jnp.bfloat16
    return pl.pallas_call(
        block_kernel,
        out_shape=jax.ShapeDtypeStruct((1, SLOTS, SLOTS), bf16),
        in_specs=[
            pl.BlockSpec(memory_space=vmem),
            pl.BlockSpec(memory_space=vmem),
            pl.BlockSpec(memory_space=pltpu.SMEM),
            *[pl.BlockSpec(memory_space=pl.ANY)] * 8,
        ],
        out_specs=pl.BlockSpec(memory_space=vmem),
        scratch_shapes=[
            vmem((3, SLOTS, SLOTS), bf16),
            vmem((SLOTS, SLOTS), bf16),
            vmem((9, MSG, 128), bf16),
            vmem((4, Z, MSG, 128), bf16),
            vmem((Z, MSG, 128), bf16),
            vmem((4, 128, 128), bf16),
            vmem((4, 128, 128), bf16),
            vmem((4, 128, 128), bf16),
            vmem((4, 16, 128), f32),
            vmem((4, 16, 128), f32),
            vmem((1024, 128), f32),
            vmem((1024, 128), f32),
            vmem((1024, 128), f32),
            vmem((Z, 128, 128), bf16),
            vmem((4, SLOTS, SLOTS), bf16),
            vmem((4, SLOTS, D), bf16),
            vmem((D, D), bf16),
            vmem((D, D), bf16),
            vmem((SLOTS, D), bf16),
            vmem((CLIPS, 4, D), f32),
            vmem((SLOTS, D), f32),
            vmem((SLOTS, D), bf16),
            vmem((SLOTS, D), bf16),
            vmem((3, SLOTS, 128), bf16),
            vmem((2, 3, SLOTS, 128), f32),
            vmem((4, 3, HALF, 128), bf16),
            vmem((2, 3, HALF, 128), bf16),
            vmem((2, 2, 3, HALF, 128), bf16),
            vmem((2, HALF, SLOTS), f32),
            vmem((2, HALF, SLOTS), f32),
            vmem((SLOTS, HALF), bf16),
            vmem((SLOTS, SLOTS), bf16),
            vmem((3, SLOTS, 128), bf16),
            vmem((3, SLOTS, 128), bf16),
            vmem((3, SLOTS, 128), bf16),
            dma((8,)),
            *[dma((Z,))] * 4,
            *[dma((3, Z))] * 2,
            *[dma((4,))] * 6,
            *[dma((Z,))] * 2,
            *[dma((4,))] * 4,
            *[dma((4, 2))] * 2,
            *[dma((2, 3))] * 2,
            dma((4, 3)),
            dma((2, 2, 3)),
            *[dma((1,))] * 2,
            *[dma((3, Z))] * 2,
            *[dma((3, Y))] * 2,
        ],
        compiler_params=pltpu.CompilerParams(
            collective_id=0, has_side_effects=True, vmem_limit_bytes=56 * 2**20
        ),
        name="guided_block",
    )(clips, owners, guide_scale, *arrays)


def shards(
    queries, keys, values, residual, w_out, w_up, w_down, modulation, guide_scale, slot_clip, owner
):
    return block(
        slot_clip,
        owner.reshape(SLOTS),
        guide_scale,
        queries,
        keys,
        values,
        residual,
        modulation,
        w_out,
        w_up,
        w_down,
    )


def solution(mesh):
    placed = (
        P("cfg", "seq", "blk"),
        P("cfg", "seq", "blk"),
        P("cfg", "seq", "blk"),
        P("cfg", "seq", None),
        P("blk", None),
        P(None, "blk"),
        P("blk", None),
        P(),
        P(),
        P("seq"),
        P("seq", None),
    )
    return jax.shard_map(
        shards, mesh=mesh, in_specs=placed, out_specs=P("cfg", "seq", "blk"), check_vma=False
    )
```
